32 devices in a mesh: dp: 4 (over x, core), ctx: 8 (over z, y).
Axes of the slice: x: 2, y: 2, z: 4, core: 2. Of those that a mesh axis runs over, the one named last changes fastest.
Arguments:
- tokens: bfloat16 [4, 1024, 1024], P('dp', 'ctx'), may hold values from -6 to 6
- cotangent: bfloat16 [4, 1024, 1024], P('dp', 'ctx'), may hold values from -6 to 6
- domain_ids: int32 [4], P('dp'), may hold values from 0 to 7
- domain_weights: float32 [8], replicated, may hold values from 0.25 to 4
- stretch_offsets: int32 [4, 8], P('dp', 'ctx'), may hold values from 0 to 7, each once within a row
- gain_attn: bfloat16 [1024], P(('dp', 'ctx')), may hold values from 0.099609375 to 1.8984375
- gain_ffn: bfloat16 [1024], P(('dp', 'ctx')), may hold values from 0.099609375 to 1.8984375
- w_query: bfloat16 [1024, 1024], P(('dp', 'ctx')), may hold values from -0.1875 to 0.1875
- w_latent: bfloat16 [1024, 512], P(('dp', 'ctx')), may hold values from -0.1875 to 0.1875
- w_upkey: bfloat16 [512, 512], P(('dp', 'ctx')), may hold values from -0.375 to 0.375
- w_upvalue: bfloat16 [512, 512], P(('dp', 'ctx')), may hold values from -0.375 to 0.375
- w_out: bfloat16 [1024, 1024], P(('dp', 'ctx')), may hold values from -4 to 4
- w_gate: bfloat16 [1024, 2816], P(('dp', 'ctx')), may hold values from -0.1875 to 0.1875
- w_up: bfloat16 [1024, 2816], P(('dp', 'ctx')), may hold values from -0.1875 to 0.1875
- w_down: bfloat16 [2816, 1024], P(('dp', 'ctx')), may hold values from -0.109375 to 0.109375
Outputs:
- output: bfloat16 [4, 1024, 1024], P('dp', 'ctx')
- grad_tokens: bfloat16 [4, 1024, 1024], P('dp', 'ctx')
- grad_gain_attn: float32 [1024], P(('dp', 'ctx'))
- grad_gain_ffn: float32 [1024], P(('dp', 'ctx'))
- grad_query: float32 [1024, 1024], P(('dp', 'ctx'))
- grad_latent: float32 [1024, 512], P(('dp', 'ctx'))
- grad_upkey: float32 [512, 512], P(('dp', 'ctx'))
- grad_upvalue: float32 [512, 512], P(('dp', 'ctx'))
- grad_out: float32 [1024, 1024], P(('dp', 'ctx'))
- grad_gate: float32 [1024, 2816], P(('dp', 'ctx'))
- grad_up: float32 [1024, 2816], P(('dp', 'ctx'))
- grad_down: float32 [2816, 1024], P(('dp', 'ctx'))
The draws below stay inside these ranges and needn't reach their ends.
Inputs may be any that keep to these rules, and one draw needn't show every extreme that they name: Each row stretch_offsets[s] is a permutation: the ctx indices hold the blocks of 128 positions of sequence s in this order.
All inputs are finite; a program needn't handle non-finite values.
Results may differ from the reference program's by a relative error of at most 0.02.
Values may be sent and summed in bfloat16 or wider, within the bound.
No kernel may reach another device: no remote copies, remote signals or barrier semaphores. Data moves between devices by JAX's collectives and lax.ppermute only.
A program may use at most 192 MiB of HBM per device.

```python
import math
import jax
import jax.numpy as jnp
from jax import lax

D = 1024
HEAD = 64
LATENT = 256
FF = 2816
DOMAINS = 8
STRETCH = 128
HPG = 8
QDIM = 1024
LEN = 1024
SEQS = 4
N_CTX = 8


def touch_ends(result, stream_key, smallest, high):
    shape = result.shape
    spot = [jax.random.randint(jax.random.fold_in(stream_key, axis), (), 0, shape[axis]) for axis in range(len(shape))]
    result = result.at[tuple(spot)].set(smallest)
    longest = shape.index(max(shape))
    spot[longest] = (spot[longest] + 1) % shape[longest]
    return result.at[tuple(spot)].set(high)


def shard_levels(own_key, extent, cuts, low, high):
    def one(position, blocks):
        heights = jax.random.uniform(jax.random.fold_in(jax.random.fold_in(own_key, 6), position), (blocks,), jnp.float32, low / len(cuts), high / len(cuts))
        return jnp.repeat(jnp.exp(heights), extent[position] // blocks).reshape((-1,) + (1,) * (len(extent) - position - 1))

    level = one(*cuts[0])
    for cut in cuts[1:]:
        level = level * one(*cut)
    return level


def noise(stream_key, shape, width, bound, pieces=(), held_as=jnp.bfloat16):
    loudness = shard_levels(stream_key, shape, pieces, -0.22, 0.18) if pieces else 1.0
    drawn = jax.random.normal(stream_key, shape, jnp.float32) * width * loudness
    return jnp.minimum(jnp.maximum(drawn, -bound), bound).astype(held_as)


def setup_inputs(seed: int = 0) -> dict:
    key_list = jax.random.split(jax.random.key(seed), 16)
    return {
        "tokens": noise(key_list[0], (SEQS, LEN, D), 1.0, 6.0, ((0, 4), (1, 8))),
        "cotangent": noise(key_list[1], (SEQS, LEN, D), 1.0, 6.0, ((0, 4), (1, 8))),
        "domain_ids": touch_ends(jax.random.randint(key_list[2], (SEQS,), 0, DOMAINS), jax.random.fold_in(key_list[2], 1), 0, DOMAINS - 1).astype(jnp.int32),
        "domain_weights": jnp.clip(jnp.exp(jax.random.uniform(key_list[3], (DOMAINS,), jnp.float32, math.log(0.25), math.log(4.0))), 0.25, 4.0),
        "stretch_offsets": jax.vmap(lambda own: jax.random.permutation(own, N_CTX))(jax.random.split(key_list[4], SEQS)).reshape((SEQS, N_CTX)).astype(jnp.int32),
        "gain_attn": jnp.clip(1.0 + 0.18 * jax.random.normal(key_list[5], (D,), jnp.float32), 0.099609375, 1.8984375).astype(jnp.bfloat16),
        "gain_ffn": jnp.clip(1.0 + 0.18 * jax.random.normal(key_list[6], (D,), jnp.float32), 0.099609375, 1.8984375).astype(jnp.bfloat16),
        "w_query": noise(key_list[7], (D, QDIM), D ** -0.5, 0.1875, ((0, 32),)),
        "w_latent": noise(key_list[8], (D, 2 * LATENT), D ** -0.5, 0.1875, ((0, 32),)),
        "w_upkey": noise(key_list[9], (2 * LATENT, HPG * HEAD), LATENT ** -0.5, 0.375, ((0, 32),)),
        "w_upvalue": noise(key_list[10], (2 * LATENT, HPG * HEAD), LATENT ** -0.5, 0.375, ((0, 32),)),
        "w_out": noise(key_list[11], (QDIM, D), (max(1, LEN // 512)) ** -0.5, 4.0, ((0, 32),)),
        "w_gate": noise(key_list[12], (D, FF), D ** -0.5, 0.1875, ((0, 32),)),
        "w_up": noise(key_list[13], (D, FF), D ** -0.5, 0.1875, ((0, 32),)),
        "w_down": noise(key_list[14], (FF, D), FF ** -0.5, 0.109375, ((0, 32),)),
    }


@jax.custom_vjp
def low(v):
    return lax.optimization_barrier(v.astype(jnp.bfloat16)).astype(jnp.float32)

@jax.custom_vjp
def low_back(v):
    return v

def low_keep(v):
    return (low(v), None)

def low_pass(kept, grad):
    return (grad,)

def back_keep(v):
    return (v, None)

def back_low(kept, grad):
    return (low(grad),)
low.defvjp(low_keep, low_pass)
low_back.defvjp(back_keep, back_low)
HIGHEST = lax.Precision.HIGHEST
EPS = 1e-06
SCALE = 0.125

def multiply_high(left, right):
    return jnp.dot(left, right, precision=HIGHEST)

def norm_rows(values, gain):
    return values * lax.rsqrt(lax.optimization_barrier(jnp.mean(values * values, -1, keepdims=True)) + EPS) * gain

def layer(x_rows, positions, params):
    gain_one, gain_two, query_w, latent_w, upkey_w, upvalue_w, out_w, gate_w, up_w, down_w = params
    normed_one = low(norm_rows(x_rows, gain_one))
    queries = low_back(low(multiply_high(normed_one, query_w)))
    latent = low_back(low(multiply_high(normed_one, latent_w)))
    upkey_heads = upkey_w.reshape(2, LATENT, HPG, HEAD)
    upvalue_heads = upvalue_w.reshape(2, LATENT, HPG, HEAD)
    query_latent = low_back(low(jnp.einsum('tgje,glje->tgjl', queries.reshape(LEN, 2, HPG, HEAD), upkey_heads, precision=HIGHEST)))
    keys = latent.reshape(LEN, 2, LATENT)
    block_rows = min(512, LEN)
    block_count = LEN // block_rows

    def attend(inputs):
        query_block, position_block = inputs
        scores = low_back(jnp.einsum('qgjl,kgl->gjqk', query_block, keys, precision=HIGHEST) * SCALE)
        allowed = position_block[:, None] >= positions[None, :]
        scores = jnp.where(allowed[None, None], scores, -1e+30)
        weights_p = low(jax.nn.softmax(scores, axis=-1))
        return low_back(low(jnp.einsum('gjqk,kgl->qgjl', weights_p, keys, precision=HIGHEST)))
    mixed_latent = lax.map(jax.checkpoint(attend), (query_latent.reshape(block_count, block_rows, 2, HPG, LATENT), positions.reshape(block_count, block_rows)))
    mixed_latent = mixed_latent.reshape(LEN, 2, HPG, LATENT)
    values = low_back(low(jnp.einsum('qgjl,glje->qgje', mixed_latent, upvalue_heads, precision=HIGHEST).reshape(LEN, QDIM)))
    middle = x_rows + low_back(multiply_high(values, out_w))
    normed_two = low(norm_rows(middle, gain_two))
    gate_pre = low_back(multiply_high(normed_two, gate_w))
    up_pre = low_back(multiply_high(normed_two, up_w))
    hidden = low(jax.nn.silu(gate_pre) * up_pre)
    return middle + low_back(multiply_high(hidden, down_w))

def add_trees(first, second):
    return tuple((left + right for left, right in zip(first, second)))

def reference(tokens, cotangent, domain_ids, domain_weights, stretch_offsets, gain_attn, gain_ffn, w_query, w_latent, w_upkey, w_upvalue, w_out, w_gate, w_up, w_down):
    params = tuple((weight.astype(jnp.float32) for weight in (gain_attn, gain_ffn, w_query, w_latent, w_upkey, w_upvalue, w_out, w_gate, w_up, w_down)))
    match = domain_ids[:, None] == jnp.arange(DOMAINS, dtype=jnp.int32)[None, :]
    seq_scale = lax.optimization_barrier(jnp.sum(jnp.where(match, domain_weights[None, :], jnp.zeros_like(domain_weights)[None, :]), -1))
    within = jnp.arange(STRETCH, dtype=jnp.int32)
    positions = (stretch_offsets.astype(jnp.int32)[:, :, None] * STRETCH + within[None, None, :]).reshape(SEQS, LEN)

    def one_sequence(totals, inputs):
        seq_tokens, seq_cot, seq_pos, seq_weight = inputs

        def forward(x_rows, weights):
            return layer(x_rows, seq_pos, weights)
        out_rows, pull = jax.vjp(forward, seq_tokens.astype(jnp.float32), params)
        d_rows, d_params = pull(seq_cot.astype(jnp.float32) * seq_weight)
        return (add_trees(totals, d_params), (out_rows.astype(jnp.bfloat16), d_rows.astype(jnp.bfloat16)))
    zeros = tuple((jnp.zeros(weight.shape, jnp.float32) for weight in params))
    totals, (outputs, d_tokens) = lax.scan(one_sequence, zeros, (tokens, cotangent, positions, seq_scale))
    return (outputs, d_tokens, totals[0], totals[1], totals[2], totals[3], totals[4], totals[5], totals[6], totals[7], totals[8], totals[9])
```

```python
import functools
import itertools

import jax
import jax.numpy as jnp
from jax import lax
from jax.experimental import pallas as pl
from jax.experimental.pallas import tpu as pltpu
from jax.sharding import PartitionSpec as P

HEADS = 16
HEAD = 64
LATENT = 256
DOMAINS = 8
EPS = 1e-06
SCALE = 0.125
MASKED = -1e30
AXES = ("dp", "ctx")
BF16 = jnp.bfloat16
F32 = jnp.float32
INFO = 8
VMEM_BYTES = 56 * 1024 * 1024


def product(left, right):
    return jnp.dot(left, right, preferred_element_type=F32)


def contract_rows(left, right):
    return lax.dot_general(left, right, (((0,), (0,)), ((), ())), preferred_element_type=F32)


def times_transposed(left, right):
    return lax.dot_general(left, right, (((1,), (1,)), ((), ())), preferred_element_type=F32)


def inverse_rms(rows):
    return lax.rsqrt(jnp.mean(rows * rows, -1, keepdims=True) + EPS)


def norm_back(rows, gain, grad):
    r = inverse_rms(rows)
    grad_gain = jnp.sum(grad * rows * r, 0)
    scaled = grad * gain
    mean = jnp.mean(scaled * rows, -1, keepdims=True)
    return r * scaled - rows * (r * r * r * mean), grad_gain


def groups_of(spots):
    groups = {}
    for n, (i, j, r, k) in enumerate(spots):
        groups.setdefault((i, r, k), []).append((j, n))
    return [(key, [n for _, n in sorted(found)]) for key, found in groups.items()]


def block_numbers(own):
    return jnp.arange(own.shape[0], dtype=own.dtype)


def permute_blocks(chosen, stack):
    out = product(chosen.astype(BF16), stack.reshape(stack.shape[0], -1)).astype(BF16)
    return out.reshape(-1, *stack.shape[1:])


def place_blocks(pieces, blocks, order, shapes):
    flat = [(o, *spot) for o, spots in enumerate(blocks) for spot in spots]
    if any(rows % 8 for rows, _ in shapes):
        made, at = [], 0
        for (rows, columns), spots in zip(shapes, blocks):
            groups = groups_of(spots)
            stack = jnp.concatenate([pieces[i][:, r : r + rows, k : k + columns] for (i, r, k), _ in groups])
            own = order[jnp.asarray([at + n for _, ns in groups for n in ns])]
            made.append(permute_blocks(own[None, :] == block_numbers(own)[:, None], stack).reshape(-1, columns))
            at += len(spots)
        return made

    def kernel(order_ref, *refs):
        sources, targets = refs[: len(pieces)], refs[len(pieces) :]
        for n, (o, i, j, r, k) in enumerate(flat):
            rows, columns = shapes[o]
            targets[o][order_ref[n]] = sources[i][j, r : r + rows, k : k + columns]

    made = pl.pallas_call(
        kernel,
        out_shape=[
            jax.ShapeDtypeStruct((len(spots), rows, columns), BF16)
            for (rows, columns), spots in zip(shapes, blocks)
        ],
        in_specs=[pl.BlockSpec(memory_space=pltpu.SMEM)]
        + [pl.BlockSpec(memory_space=pltpu.VMEM)] * len(pieces),
        out_specs=[pl.BlockSpec(memory_space=pltpu.VMEM)] * len(shapes),
        compiler_params=pltpu.CompilerParams(vmem_limit_bytes=VMEM_BYTES),
        name="place_blocks",
    )(order, *pieces)
    return [whole.reshape(-1, whole.shape[-1]) for whole in made]


def cut_blocks(matrices, blocks, order, shapes, piece_shapes):
    flat = [(o, *spot) for o, spots in enumerate(blocks) for spot in spots]
    if any(rows % 8 for rows, _ in shapes):
        bands, at = [{} for _ in piece_shapes], 0
        for (rows, columns), spots, matrix in zip(shapes, blocks, matrices):
            grid = matrix.reshape(len(spots), rows, columns)
            for (i, r, k), ns in groups_of(spots):
                own = order[jnp.asarray([at + n for n in ns])]
                chosen = own[:, None] == jnp.arange(len(spots), dtype=own.dtype)[None, :]
                bands[i].setdefault(r, {})[k] = permute_blocks(chosen, grid)
            at += len(spots)
        return [
            jnp.concatenate(
                [jnp.concatenate([row[k] for k in sorted(row)], 2) for _, row in sorted(band.items())], 1
            )
            for band in bands
        ]

    def kernel(order_ref, *refs):
        sources, targets = refs[: len(matrices)], refs[len(matrices) :]
        for n, (o, i, j, r, k) in enumerate(flat):
            rows, columns = shapes[o]
            targets[i][j, r : r + rows, k : k + columns] = sources[o][order_ref[n]]

    grids = [matrix.reshape(-1, rows, columns) for matrix, (rows, columns) in zip(matrices, shapes)]
    return pl.pallas_call(
        kernel,
        out_shape=[jax.ShapeDtypeStruct(shape, BF16) for shape in piece_shapes],
        in_specs=[pl.BlockSpec(memory_space=pltpu.SMEM)]
        + [pl.BlockSpec(memory_space=pltpu.VMEM)] * len(matrices),
        out_specs=[pl.BlockSpec(memory_space=pltpu.VMEM)] * len(piece_shapes),
        compiler_params=pltpu.CompilerParams(vmem_limit_bytes=VMEM_BYTES),
        name="cut_blocks",
    )(order, *grids)


def pair_scores(query_latent, keys, query_pos, key_pos):
    scores = times_transposed(query_latent, keys) * SCALE
    both = jnp.concatenate([query_pos, query_pos], 0)
    return jnp.where(both >= key_pos, scores, MASKED)


def attend_kernel(q_ref, uk_ref, uv_ref, keys_ref, qpos_ref, kpos_ref, ql_ref, mixed_ref, lse_ref, values_ref):
    q, uk, uv, keys = q_ref[0], uk_ref[...], uv_ref[...], keys_ref[0]
    rows = q.shape[0]
    ql = jnp.concatenate(
        [times_transposed(q[:, k : k + HEAD], uk[:, k : k + HEAD]) for k in (0, HEAD)], 0
    ).astype(BF16)
    scores = pair_scores(ql, keys, qpos_ref[0], kpos_ref[0])
    top = jnp.max(scores, -1, keepdims=True)
    terms = jnp.exp(scores - top)
    total = jnp.sum(terms, -1, keepdims=True)
    probs = (terms * (1.0 / total)).astype(BF16)
    mixed = product(probs, keys).astype(BF16)
    ql_ref[0, 0] = ql
    mixed_ref[0, 0] = mixed
    lse_ref[0, 0] = top + jnp.log(total)
    values_ref[0] = jnp.concatenate(
        [product(mixed[:rows], uv[:, :HEAD]), product(mixed[rows:], uv[:, HEAD:])], 1
    ).astype(BF16)


def attend_back_kernel(
    q_ref, ql_ref, mixed_ref, lse_ref, dval_ref, uk_ref, uv_ref, keys_ref, qpos_ref, kpos_ref,
    dq_ref, guk_ref, guv_ref, *rest,
):
    dkeys_refs, (keys_acc, uk_acc, uv_acc) = rest[:-3], rest[-3:]
    seq, pair = pl.program_id(0), pl.program_id(1)
    q, ql, mixed, dval = q_ref[0], ql_ref[0, 0], mixed_ref[0, 0], dval_ref[0]
    uk, uv, keys = uk_ref[...], uv_ref[...], keys_ref[0]
    rows = q.shape[0]
    halves = (0, HEAD)
    scores = pair_scores(ql, keys, qpos_ref[0], kpos_ref[0])
    probs = jnp.exp(scores - lse_ref[0, 0])
    dmixed = jnp.concatenate(
        [times_transposed(dval[:, k : k + HEAD], uv[:, k : k + HEAD]) for k in halves], 0
    ).astype(BF16)
    dprobs = times_transposed(dmixed, keys)
    dscores = probs * (dprobs - jnp.sum(probs * dprobs, -1, keepdims=True))
    dscores = dscores.astype(BF16) * jnp.asarray(SCALE, BF16)
    dql = product(dscores, keys).astype(BF16)
    dkeys = contract_rows(dscores, ql) + contract_rows(probs.astype(BF16), dmixed)

    @pl.when(pair == 0)
    def _():
        keys_acc[...] = dkeys

    @pl.when(pair > 0)
    def _():
        keys_acc[...] += dkeys

    guk = jnp.concatenate(
        [contract_rows(dql[n * rows : (n + 1) * rows], q[:, k : k + HEAD]) for n, k in enumerate(halves)], 1
    )
    guv = jnp.concatenate(
        [contract_rows(mixed[n * rows : (n + 1) * rows], dval[:, k : k + HEAD]) for n, k in enumerate(halves)], 1
    )

    @pl.when(seq == 0)
    def _():
        uk_acc[pair] = guk
        uv_acc[pair] = guv

    @pl.when(seq > 0)
    def _():
        uk_acc[pair] += guk
        uv_acc[pair] += guv

    dq_ref[0] = jnp.concatenate(
        [product(dql[n * rows : (n + 1) * rows], uk[:, k : k + HEAD]) for n, k in enumerate(halves)], 1
    ).astype(BF16)
    last = pl.num_programs(1) - 1

    @pl.when(pair == last)
    def _():
        count = dkeys_refs[0].shape[0]
        for n, ref in enumerate(dkeys_refs):
            part = keys_acc[n * count * rows : (n + 1) * count * rows, :]
            ref[:, 0] = part.reshape(count, rows, LATENT).astype(BF16)

    @pl.when((pair == last) & (seq == pl.num_programs(0) - 1))
    def _():
        for n in range(uk_acc.shape[0]):
            guk_ref[:, 2 * n * HEAD : 2 * (n + 1) * HEAD] = uk_acc[n].astype(BF16)
            guv_ref[:, 2 * n * HEAD : 2 * (n + 1) * HEAD] = uv_acc[n].astype(BF16)


def attention_specs(length, rows):
    pair = pl.BlockSpec((1, rows, 2 * HEAD), lambda s, p: (s, 0, p))
    up = pl.BlockSpec((LATENT, 2 * HEAD), lambda s, p: (0, p))
    keys = pl.BlockSpec((1, length, LATENT), lambda s, p: (s, 0, 0))
    query_pos = pl.BlockSpec((1, rows, 1), lambda s, p: (s, 0, 0))
    key_pos = pl.BlockSpec((1, 1, length), lambda s, p: (s, 0, 0))
    wide = pl.BlockSpec((1, 1, 2 * rows, LATENT), lambda s, p: (s, p, 0, 0))
    thin = pl.BlockSpec((1, 1, 2 * rows, 1), lambda s, p: (s, p, 0, 0))
    return pair, up, keys, query_pos, key_pos, wide, thin


def attend(q, uk, uv, keys, query_pos, key_pos):
    seqs, length, _ = keys.shape
    rows, pairs = q.shape[1], q.shape[2] // (2 * HEAD)
    pair, up, key, qpos, kpos, wide, thin = attention_specs(length, rows)
    flops = seqs * pairs * 2 * rows * length * LATENT * 4
    return pl.pallas_call(
        attend_kernel,
        grid=(seqs, pairs),
        in_specs=[pair, up, up, key, qpos, kpos],
        out_specs=[wide, wide, thin, pair],
        out_shape=[
            jax.ShapeDtypeStruct((seqs, pairs, 2 * rows, LATENT), BF16),
            jax.ShapeDtypeStruct((seqs, pairs, 2 * rows, LATENT), BF16),
            jax.ShapeDtypeStruct((seqs, pairs, 2 * rows, 1), F32),
            jax.ShapeDtypeStruct(q.shape, BF16),
        ],
        compiler_params=pltpu.CompilerParams(vmem_limit_bytes=VMEM_BYTES),
        cost_estimate=pl.CostEstimate(flops=flops, bytes_accessed=6 << 20, transcendentals=seqs * pairs * 2 * rows * length),
        name="attend",
    )(q, uk, uv, keys, query_pos, key_pos)


def attend_back(q, ql, mixed, lse, dval, uk, uv, keys, query_pos, key_pos, parts):
    seqs, length, _ = keys.shape
    rows, pairs = q.shape[1], q.shape[2] // (2 * HEAD)
    pair, up, key, qpos, kpos, wide, thin = attention_specs(length, rows)
    whole = pl.BlockSpec(uk.shape, lambda s, p: (0, 0))
    count = length // rows // parts
    flops = seqs * pairs * 2 * rows * length * LATENT * 10
    return pl.pallas_call(
        attend_back_kernel,
        grid=(seqs, pairs),
        in_specs=[pair, wide, wide, thin, pair, up, up, key, qpos, kpos],
        out_specs=[pair, whole, whole]
        + [pl.BlockSpec((count, 1, rows, LATENT), lambda s, p: (0, s, 0, 0))] * parts,
        out_shape=[jax.ShapeDtypeStruct(q.shape, BF16)]
        + [jax.ShapeDtypeStruct(uk.shape, BF16)] * 2
        + [jax.ShapeDtypeStruct((count, seqs, rows, LATENT), BF16)] * parts,
        scratch_shapes=[
            pltpu.VMEM((length, LATENT), F32),
            pltpu.VMEM((pairs, LATENT, 2 * HEAD), F32),
            pltpu.VMEM((pairs, LATENT, 2 * HEAD), F32),
        ],
        compiler_params=pltpu.CompilerParams(vmem_limit_bytes=VMEM_BYTES),
        cost_estimate=pl.CostEstimate(flops=flops, bytes_accessed=8 << 20, transcendentals=seqs * pairs * 2 * rows * length),
        name="attend_back",
    )(q, ql, mixed, lse, dval, uk, uv, keys, query_pos, key_pos)


class Plan:
    def __init__(self, mesh):
        self.dp, self.ctx = mesh.shape["dp"], mesh.shape["ctx"]
        self.count = self.dp * self.ctx
        self.core = self.ctx
        self.cross = 2 * self.ctx
        top = self.count // 2
        bits = [1 << n for n in range(self.count.bit_length() - 1)]
        ctx_bits = [b for b in bits if b < self.ctx]
        self.half_bits = [b for b in bits if b != self.core]
        self.split_bits = [self.core, self.cross]
        self.quarter_bits = [b for b in bits if b not in self.split_bits]
        self.ctx_bits = ctx_bits
        self.top = top

    def swap(self, value, mask):
        return lax.ppermute(value, AXES, [(n, n ^ mask) for n in range(self.count)])

    def swap_bits(self, number, first, second):
        if first == second:
            return number
        one, two = (number // first) % 2, (number // second) % 2
        return number + (two - one) * first + (one - two) * second

    def deal(self, value, pairs):
        table = []
        for n in range(self.count):
            m = n
            for first, second in pairs:
                m = self.swap_bits(m, first, second)
            table.append((n, m))
        if all(a == b for a, b in table):
            return value
        return lax.ppermute(value, AXES, table)


def masks_of(bits):
    out = [0]
    for bit in bits:
        out = out + [m ^ bit for m in out]
    return out


def gather(plan, value, far, second, first, groups):
    done = [([m], value[None] if m == 0 else plan.swap(value, m)[None]) for m in masks_of(far)]
    for bit in (second, first):
        size = -(-len(done) // groups)
        sent = []
        for at in range(0, len(done), size):
            some = done[at : at + size]
            masks = [m for ms, _ in some for m in ms]
            stack = some[0][1] if len(some) == 1 else jnp.concatenate([a for _, a in some])
            sent.append(([m ^ bit for m in masks], plan.swap(stack, bit)))
        done = done + sent
    return done


def reduce_order(far, second, first):
    base = masks_of(far)
    return [[m ^ one ^ two for m in base] for one in (0, first) for two in (0, second)]


def reduce(plan, stacks, far, second, first):
    keep0, keep1, send0, send1 = stacks
    got1 = plan.swap(send1, first)
    got0 = plan.swap(send0, first)
    part1 = (keep1.astype(F32) + got1.astype(F32)).astype(BF16)
    got = plan.swap(part1, second)
    part = (keep0.astype(F32) + got0.astype(F32) + got.astype(F32)).astype(BF16)
    total = part[0].astype(F32)
    for n, mask in enumerate(masks_of(far)):
        if n:
            total = total + plan.swap(part[n], mask).astype(F32)
    return total


def per_device(plan, tokens, cotangent, domain_ids, domain_weights, stretch_offsets, gain_attn, gain_ffn,
               w_query, w_latent, w_upkey, w_upvalue, w_out, w_gate, w_up, w_down):
    _, rows, width = tokens.shape
    me = lax.axis_index("dp") * plan.ctx + lax.axis_index("ctx")
    core = (me // plan.core) % 2
    core_bit, cross_bit = plan.core, plan.cross
    count = plan.count
    shard = w_query.shape[0]
    up_shard = w_upkey.shape[0]
    down_shard = w_down.shape[0]
    half = w_query.shape[1] // 2
    latent_half = w_latent.shape[1] // 2
    quarter = w_gate.shape[1] // 4
    ctx_first, ctx_second, *ctx_far = plan.ctx_bits
    x_bit = plan.half_bits[-1]
    half_far = [b for b in plan.half_bits if b not in (x_bit, ctx_first)]
    quarter_far = [b for b in plan.quarter_bits if b not in (ctx_first, ctx_second)]

    def halves(value, size):
        low, high = value[:, :size], value[:, size:]
        return jnp.where(core == 0, low, high), jnp.where(core == 0, high, low)

    query_own, query_other = halves(w_query, half)
    latent_own, latent_other = halves(w_latent, latent_half)
    span = half + latent_half
    info = jnp.concatenate([gain_attn, gain_ffn, stretch_offsets[0].astype(BF16)])
    info = jnp.pad(info[None], ((0, INFO - 1), (0, span - info.shape[0])))
    mine = jnp.concatenate([jnp.concatenate([query_own, latent_own], 1), info])
    other = jnp.concatenate([jnp.concatenate([query_other, latent_other], 1), info])
    band = shard + INFO
    first_message = jnp.concatenate([mine, plan.swap(other, core_bit)])
    second_message = plan.deal(
        jnp.concatenate([jnp.concatenate([w_upkey, w_upvalue], 1).reshape(-1, width), w_out]),
        [(plan.top, core_bit)],
    )
    split_masks = masks_of(plan.split_bits)
    split = (me // core_bit) % 2 + 2 * ((me // cross_bit) % 2)
    columns = jnp.concatenate([w_gate, w_up]).reshape(2 * shard, 4, quarter).transpose(1, 0, 2)

    def quarter_of(mask_index):
        return lax.dynamic_index_in_dim(columns, split ^ mask_index, 0, keepdims=False)

    third_message = jnp.concatenate(
        [quarter_of(0)] + [plan.swap(quarter_of(n), m) for n, m in enumerate(split_masks) if n]
    )
    fourth_message = plan.deal(w_down, [(plan.top, cross_bit), (plan.top // 2, core_bit)])

    tokens_two = jnp.concatenate([tokens[0], plan.swap(tokens[0], core_bit)])
    x_two = tokens_two.astype(F32)

    half_stages = (half_far, ctx_first, x_bit)
    quarter_stages = (quarter_far, ctx_second, ctx_first)
    first_pieces = gather(plan, first_message, *half_stages, 4)
    second_pieces = gather(plan, second_message, *half_stages, 4)
    third_pieces = gather(plan, third_message, *quarter_stages, 4)
    fourth_pieces = gather(plan, fourth_message, *quarter_stages, 4)

    def spots(pieces):
        return [(i, j, m) for i, (masks, _) in enumerate(pieces) for j, m in enumerate(masks)]

    query_blocks, latent_blocks, order = [], [], []
    for i, j, m in spots(first_pieces):
        for b in (0, 1):
            query_blocks.append((i, j, b * band, 0))
            latent_blocks.append((i, j, b * band, half))
            order.append(me ^ (m ^ b * core_bit))
    query_full, latent_full = place_blocks(
        [a for _, a in first_pieces], [query_blocks, latent_blocks], jnp.stack(order + order),
        [(shard, half), (shard, latent_half)],
    )

    def owner_half(m):
        return plan.swap_bits(me ^ m, plan.top, core_bit) % (count // 2)

    up_rows = 2 * up_shard * w_upkey.shape[1] // width
    second_stacks = [a for _, a in second_pieces]
    out_blocks = [(i, j, up_rows, 0) for i, j, m in spots(second_pieces)]
    order_half = jnp.stack([owner_half(m) for _, _, m in spots(second_pieces)])
    pair_width = w_upkey.shape[1]
    upkey_blocks = [(i, j, 0, 0) for i, j, m in spots(second_pieces)]
    upvalue_blocks = [(i, j, 0, pair_width) for i, j, m in spots(second_pieces)]
    upkey_full, upvalue_full, out_full = place_blocks(
        second_stacks, [upkey_blocks, upvalue_blocks, out_blocks],
        jnp.concatenate([order_half] * 3),
        [(up_shard, pair_width), (up_shard, pair_width), (shard, width)],
    )

    gate_blocks, up_blocks, order = [], [], []
    for i, j, m in spots(third_pieces):
        for n, s in enumerate(split_masks):
            gate_blocks.append((i, j, n * 2 * shard, 0))
            up_blocks.append((i, j, n * 2 * shard + shard, 0))
            order.append(me ^ (m ^ s))
    order_columns = jnp.stack(order + order)
    gate_full, up_full = place_blocks(
        [a for _, a in third_pieces], [gate_blocks, up_blocks], order_columns, [(shard, quarter)] * 2
    )

    def owner_quarter(m):
        source = plan.swap_bits(me ^ m, plan.top // 2, core_bit)
        return plan.swap_bits(source, plan.top, cross_bit) % (count // 4)

    down_blocks = [(i, j, 0, 0) for i, j, m in spots(fourth_pieces)]
    order_down = jnp.stack([owner_quarter(m) for _, _, m in spots(fourth_pieces)])
    (down_full,) = place_blocks(
        [a for _, a in fourth_pieces], [down_blocks], order_down, [(down_shard, width)]
    )

    rows_info = jnp.concatenate(
        [a[:, shard :: band, : 2 * shard + 1] for _, a in first_pieces]
    )
    masks_info = [m for _, _, m in spots(first_pieces)]
    number = jnp.stack([jnp.stack([me ^ m, me ^ m ^ core_bit]) for m in masks_info]).reshape(-1)
    chosen = (number[:, None] == jnp.arange(count)[None, :]).astype(BF16)
    gains = contract_rows(chosen, rows_info[..., : 2 * shard].reshape(count, 2 * shard))
    gain_one = gains[:, :shard].reshape(width)
    gain_two = gains[:, shard:].reshape(width)
    ctx_masks = sum(reduce_order(ctx_far, ctx_second, ctx_first), [])
    offsets = jnp.stack(
        [rows_info[masks_info.index(m), :, 2 * shard] for m in ctx_masks], 1
    ).astype(jnp.int32)
    within = jnp.arange(rows, dtype=jnp.int32)
    key_pos = (offsets[:, :, None] * rows + within).reshape(2, 1, -1)
    query_pos = (offsets[:, :1] * rows + within)[:, :, None]

    normed_one = (x_two * inverse_rms(x_two) * gain_one).astype(BF16)
    latent = product(normed_one, latent_full).astype(BF16)
    latent_message = latent.reshape(2, rows, latent_half)
    key_pieces = gather(plan, latent_message, ctx_far, ctx_second, ctx_first, 4)
    key_of = {m: a[j] for masks, a in key_pieces for j, m in enumerate(masks)}
    keys = jnp.concatenate([key_of[m] for m in ctx_masks], 1)
    queries = product(normed_one, query_full).astype(BF16).reshape(2, rows, half)
    query_latent, mixed, lse, values = attend(queries, upkey_full, upvalue_full, keys, query_pos, key_pos)
    values = values.reshape(2 * rows, half)
    shares = product(values, out_full)
    x_own = x_two[:rows]
    middle = x_own + shares[:rows] + plan.swap(shares[rows:], core_bit)

    def spread(value):
        near = plan.swap(value, core_bit)
        across = plan.swap(value, cross_bit)
        return jnp.concatenate([value, near, across, plan.swap(across, core_bit)])

    def collect(shares):
        parts = shares.reshape(4, rows, width)
        got = plan.swap(jnp.stack([parts[1], parts[3]]), core_bit)
        across = plan.swap((parts[2] + got[1]).astype(BF16), cross_bit)
        return parts[0] + got[0] + across.astype(F32)

    match = domain_ids[:, None] == jnp.arange(DOMAINS, dtype=jnp.int32)[None, :]
    scale = jnp.sum(jnp.where(match, domain_weights[None, :], 0.0))
    dlayer = cotangent[0].astype(F32) * scale
    dy = spread(dlayer.astype(BF16))

    normed_two = spread((middle * inverse_rms(middle) * gain_two).astype(BF16))
    gate = product(normed_two, gate_full)
    up = product(normed_two, up_full)
    sigmoid = jax.nn.sigmoid(gate)
    silu = gate * sigmoid
    hidden = (silu * up).astype(BF16)
    dhidden = times_transposed(dy, down_full)
    dgate = (dhidden * up * (sigmoid * (1.0 + gate * (1.0 - sigmoid)))).astype(BF16)
    dup = (dhidden * silu).astype(BF16)
    dnormed_two = collect(times_transposed(dgate, gate_full) + times_transposed(dup, up_full))
    grad_gate = contract_rows(normed_two, dgate).astype(BF16)
    grad_up = contract_rows(normed_two, dup).astype(BF16)
    grad_down = contract_rows(hidden, dy).astype(BF16)
    output = (middle + collect(product(hidden, down_full))).astype(BF16)[None]

    quarter_order = reduce_order(*quarter_stages)
    blocks, order = [], []
    for i, masks in enumerate(quarter_order):
        for j, m in enumerate(masks):
            blocks.append((i, j, 0, 0))
            order.append(owner_quarter(m))
    down_stacks = cut_blocks(
        [grad_down], [blocks], jnp.stack(order), [(down_shard, width)],
        [(len(masks), down_shard, width) for masks in quarter_order],
    )
    down_sum = reduce(plan, down_stacks, *quarter_stages)
    grad_w_down = plan.deal(down_sum, [(plan.top // 2, core_bit), (plan.top, cross_bit)])

    gate_blocks, up_blocks, order = [], [], []
    for i, masks in enumerate(quarter_order):
        for j, m in enumerate(masks):
            for n, s in enumerate(split_masks):
                gate_blocks.append((i, j, n * 2 * shard, 0))
                up_blocks.append((i, j, n * 2 * shard + shard, 0))
                order.append(me ^ (m ^ s))
    column_stacks = cut_blocks(
        [grad_gate, grad_up], [gate_blocks, up_blocks], jnp.stack(order + order), [(shard, quarter)] * 2,
        [(len(masks), 8 * shard, quarter) for masks in quarter_order],
    )
    column_sum = reduce(plan, column_stacks, *quarter_stages).reshape(4, 2 * shard, quarter)
    got = [column_sum[0]] + [
        plan.swap(column_sum[n].astype(BF16), m).astype(F32) for n, m in enumerate(split_masks) if n
    ]
    got = jnp.stack(got)
    grad_columns = jnp.concatenate(
        [lax.dynamic_index_in_dim(got, split ^ n, 0, keepdims=False) for n in range(4)], 1
    )
    grad_w_gate, grad_w_up = grad_columns[:shard], grad_columns[shard:]

    dmiddle_norm, grad_gain_two = norm_back(middle, gain_two, dnormed_two)
    dmiddle = dlayer + dmiddle_norm
    dm = dmiddle.astype(BF16)
    dm_two = jnp.concatenate([dm, plan.swap(dm, core_bit)])
    grad_out = contract_rows(values, dm_two).astype(BF16)
    dvalues = times_transposed(dm_two, out_full).astype(BF16).reshape(2, rows, half)
    dqueries, grad_upkey, grad_upvalue, *dkeys = attend_back(
        queries, query_latent, mixed, lse, dvalues, upkey_full, upvalue_full, keys, query_pos, key_pos, 4
    )
    dlatent = reduce(plan, dkeys, ctx_far, ctx_second, ctx_first).astype(BF16).reshape(2 * rows, latent_half)
    dqueries = dqueries.reshape(2 * rows, half)
    shares = times_transposed(dqueries, query_full) + times_transposed(dlatent, latent_full)
    dnormed_one = shares[:rows] + plan.swap(shares[rows:], core_bit)
    dx_norm, grad_gain_one = norm_back(x_own, gain_one, dnormed_one)
    grad_tokens = (dmiddle + dx_norm).astype(BF16)[None]

    half_order = reduce_order(*half_stages)
    blocks, order = [], []
    for i, masks in enumerate(half_order):
        for j, m in enumerate(masks):
            blocks.append((i, j))
            order.append(owner_half(m))
    second_stacks = cut_blocks(
        [grad_upkey, grad_upvalue, grad_out],
        [[(i, j, 0, 0) for i, j in blocks], [(i, j, 0, pair_width) for i, j in blocks],
         [(i, j, up_rows, 0) for i, j in blocks]],
        jnp.stack(order * 3),
        [(up_shard, pair_width), (up_shard, pair_width), (shard, width)],
        [(len(masks), up_rows + shard, width) for masks in half_order],
    )
    second_sum = plan.deal(reduce(plan, second_stacks, *half_stages), [(plan.top, core_bit)])
    grad_ups = second_sum[:up_rows].reshape(up_shard, 2 * pair_width)
    grad_w_out = second_sum[up_rows:]

    grad_query = contract_rows(normed_one, dqueries).astype(BF16)
    grad_latent = contract_rows(normed_one, dlatent).astype(BF16)
    gain_rows = jnp.concatenate([grad_gain_one.reshape(count, shard), grad_gain_two.reshape(count, shard)], 1)
    gain_rows = jnp.pad(gain_rows.astype(BF16)[:, None], ((0, 0), (0, INFO - 1), (0, span - 2 * shard)))
    gain_rows = gain_rows.reshape(count * INFO, span)
    query_blocks, latent_blocks, info_blocks, order = [], [], [], []
    for i, masks in enumerate(half_order):
        for j, m in enumerate(masks):
            for b in (0, 1):
                query_blocks.append((i, j, b * band, 0))
                latent_blocks.append((i, j, b * band, half))
                info_blocks.append((i, j, b * band + shard, 0))
                order.append(me ^ (m ^ b * core_bit))
    first_stacks = cut_blocks(
        [grad_query, grad_latent, gain_rows], [query_blocks, latent_blocks, info_blocks],
        jnp.stack(order * 3),
        [(shard, half), (shard, latent_half), (INFO, span)],
        [(len(masks), 2 * band, span) for masks in half_order],
    )
    first_sum = reduce(plan, first_stacks, *half_stages)
    own, got = first_sum[:band], plan.swap(first_sum[band:].astype(BF16), core_bit).astype(F32)
    low, high = jnp.where(core == 0, own, got), jnp.where(core == 0, got, own)
    grad_w_query = jnp.concatenate([low[:shard, :half], high[:shard, :half]], 1)
    grad_w_latent = jnp.concatenate([low[:shard, half:], high[:shard, half:]], 1)
    gain_sums = own[shard] + got[shard]

    return (
        output, grad_tokens, gain_sums[:shard], gain_sums[shard : 2 * shard],
        grad_w_query, grad_w_latent, grad_ups[:, :pair_width], grad_ups[:, pair_width:],
        grad_w_out, grad_w_gate, grad_w_up, grad_w_down,
    )


def solution(mesh):
    rows = P(("dp", "ctx"), None)
    vector = P(("dp", "ctx"))
    stretch = P("dp", "ctx", None)
    in_specs = (stretch, stretch, P("dp"), P(), P("dp", "ctx"), vector, vector) + (rows,) * 8
    out_specs = (stretch, stretch, vector, vector) + (rows,) * 8
    return jax.shard_map(
        functools.partial(per_device, Plan(mesh)), mesh=mesh, in_specs=in_specs, out_specs=out_specs,
        check_vma=False,
    )
```

```python
import functools
import itertools
import math

import jax
import jax.numpy as jnp
from jax import lax
from jax.experimental import pallas as pl
from jax.experimental.pallas import tpu as pltpu
from jax.sharding import PartitionSpec as P

HEADS = 16
HEAD = 64
LATENT = 256
DOMAINS = 8
EPS = 1e-06
SCALE = 0.125
MASKED = -1e30
AXES = ("dp", "ctx")
BF16 = jnp.bfloat16
F32 = jnp.float32
INFO = 8
VMEM_BYTES = 56 * 1024 * 1024


def product(left, right):
    return jnp.dot(left, right, preferred_element_type=F32)


def contract_rows(left, right):
    return lax.dot_general(left, right, (((0,), (0,)), ((), ())), preferred_element_type=F32)


def times_transposed(left, right):
    return lax.dot_general(left, right, (((1,), (1,)), ((), ())), preferred_element_type=F32)


def inverse_rms(rows):
    return lax.rsqrt(jnp.mean(rows * rows, -1, keepdims=True) + EPS)


def norm_back(rows, gain, grad):
    r = inverse_rms(rows)
    grad_gain = jnp.sum(grad * rows * r, 0)
    scaled = grad * gain
    mean = jnp.mean(scaled * rows, -1, keepdims=True)
    return r * scaled - rows * (r * r * r * mean), grad_gain


def groups_of(spots):
    groups = {}
    for n, (i, j, r, k) in enumerate(spots):
        groups.setdefault((i, r, k), []).append((j, n))
    return [(key, [n for _, n in sorted(found)]) for key, found in groups.items()]


def permute_blocks(chosen, stack):
    out = product(chosen.astype(BF16), stack.reshape(stack.shape[0], -1)).astype(BF16)
    return out.reshape(-1, *stack.shape[1:])


def bands_of(widths):
    return list(zip(widths, itertools.accumulate([0, *widths[:-1]])))


def kernel_bytes(shapes):
    return 4 * sum(math.prod(shape) for shape in shapes) + (4 << 20)


def place_blocks(pieces, blocks, orders, shapes):
    if any(rows % 8 for rows, _ in shapes):
        made = []
        for (rows, widths), bands, order in zip(shapes, blocks, orders):
            parts = []
            for (width, _), spots in zip(bands_of(widths), bands):
                groups = groups_of(spots)
                stack = jnp.concatenate([pieces[i][:, r : r + rows, k : k + width] for (i, r, k), _ in groups])
                own = jnp.stack([order[n] for _, ns in groups for n in ns])
                numbers = jnp.arange(len(spots), dtype=own.dtype)
                parts.append(permute_blocks(own[None, :] == numbers[:, None], stack))
            made.append(jnp.concatenate(parts, 2).reshape(-1, sum(widths)))
        return made

    def kernel(order_ref, *refs):
        sources, targets = refs[: len(pieces)], refs[len(pieces) :]
        first = 0
        for target, (rows, widths), bands in zip(targets, shapes, blocks):
            for (width, column), spots in zip(bands_of(widths), bands):
                for n, (i, j, r, k) in enumerate(spots):
                    target[order_ref[first + n], :, column : column + width] = sources[i][
                        j, r : r + rows, k : k + width
                    ]
            first += len(bands[0])

    out_shapes = [(len(bands[0]), rows, sum(widths)) for (rows, widths), bands in zip(shapes, blocks)]
    made = pl.pallas_call(
        kernel,
        out_shape=[jax.ShapeDtypeStruct(shape, BF16) for shape in out_shapes],
        in_specs=[pl.BlockSpec(memory_space=pltpu.SMEM)]
        + [pl.BlockSpec(memory_space=pltpu.VMEM)] * len(pieces),
        out_specs=[pl.BlockSpec(memory_space=pltpu.VMEM)] * len(shapes),
        compiler_params=pltpu.CompilerParams(
            vmem_limit_bytes=kernel_bytes(out_shapes + [p.shape for p in pieces])
        ),
        name="place_blocks",
    )(jnp.stack([n for order in orders for n in order]), *pieces)
    return [whole.reshape(-1, whole.shape[-1]) for whole in made]


def cut_blocks(matrices, blocks, orders, shapes, piece_shapes, spare=()):
    if any(rows % 8 for rows, _ in shapes):
        bands_at = [{} for _ in piece_shapes]
        for (rows, widths), bands, order, matrix in zip(shapes, blocks, orders, matrices):
            grid = matrix.reshape(len(bands[0]), rows, -1)
            for (width, column), spots in zip(bands_of(widths), bands):
                for (i, r, k), ns in groups_of(spots):
                    own = jnp.stack([order[n] for n in ns])
                    chosen = own[:, None] == jnp.arange(len(spots), dtype=own.dtype)[None, :]
                    bands_at[i].setdefault(r, {})[k] = permute_blocks(chosen, grid[:, :, column : column + width])
        for i, r, rows, k, columns in spare:
            bands_at[i].setdefault(r, {})[k] = jnp.zeros((piece_shapes[i][0], rows, columns), BF16)
        return [
            jnp.concatenate(
                [jnp.concatenate([row[k] for k in sorted(row)], 2) for _, row in sorted(band.items())], 1
            )
            for band in bands_at
        ]

    def kernel(order_ref, *refs):
        sources, targets = refs[: len(matrices)], refs[len(matrices) :]
        for i, r, rows, k, columns in spare:
            targets[i][:, r : r + rows, k : k + columns] = jnp.zeros((piece_shapes[i][0], rows, columns), BF16)
        first = 0
        for source, (rows, widths), bands in zip(sources, shapes, blocks):
            for (width, column), spots in zip(bands_of(widths), bands):
                for n, (i, j, r, k) in enumerate(spots):
                    targets[i][j, r : r + rows, k : k + width] = source[
                        order_ref[first + n], :, column : column + width
                    ]
            first += len(bands[0])

    grids = [matrix.reshape(-1, rows, matrix.shape[-1]) for matrix, (rows, _) in zip(matrices, shapes)]
    return pl.pallas_call(
        kernel,
        out_shape=[jax.ShapeDtypeStruct(shape, BF16) for shape in piece_shapes],
        in_specs=[pl.BlockSpec(memory_space=pltpu.SMEM)]
        + [pl.BlockSpec(memory_space=pltpu.VMEM)] * len(matrices),
        out_specs=[pl.BlockSpec(memory_space=pltpu.VMEM)] * len(piece_shapes),
        compiler_params=pltpu.CompilerParams(
            vmem_limit_bytes=kernel_bytes(list(piece_shapes) + [g.shape for g in grids])
        ),
        name="cut_blocks",
    )(jnp.stack([n for order in orders for n in order]), *grids)


def pair_scores(query_latent, keys, query_pos, key_pos):
    scores = times_transposed(query_latent, keys) * SCALE
    both = jnp.concatenate([query_pos, query_pos], 0)
    return jnp.where(both >= key_pos, scores, MASKED)


def attend_kernel(q_ref, uk_ref, uv_ref, keys_ref, qpos_ref, kpos_ref, ql_ref, mixed_ref, lse_ref, values_ref):
    q, uk, uv, keys = q_ref[0], uk_ref[...], uv_ref[...], keys_ref[0]
    rows = q.shape[0]
    ql = jnp.concatenate(
        [times_transposed(q[:, k : k + HEAD], uk[:, k : k + HEAD]) for k in (0, HEAD)], 0
    ).astype(BF16)
    scores = pair_scores(ql, keys, qpos_ref[0], kpos_ref[0])
    top = jnp.max(scores, -1, keepdims=True)
    terms = jnp.exp(scores - top)
    total = jnp.sum(terms, -1, keepdims=True)
    probs = (terms * (1.0 / total)).astype(BF16)
    mixed = product(probs, keys).astype(BF16)
    ql_ref[0, 0] = ql
    mixed_ref[0, 0] = mixed
    lse_ref[0, 0] = top + jnp.log(total)
    values_ref[0] = jnp.concatenate(
        [product(mixed[:rows], uv[:, :HEAD]), product(mixed[rows:], uv[:, HEAD:])], 1
    ).astype(BF16)


def attend_back_kernel(
    q_ref, ql_ref, mixed_ref, lse_ref, dval_ref, uk_ref, uv_ref, keys_ref, qpos_ref, kpos_ref,
    dq_ref, guk_ref, guv_ref, *rest,
):
    dkeys_refs, (keys_acc, uk_acc, uv_acc) = rest[:-3], rest[-3:]
    seq, pair = pl.program_id(0), pl.program_id(1)
    q, ql, mixed, dval = q_ref[0], ql_ref[0, 0], mixed_ref[0, 0], dval_ref[0]
    uk, uv, keys = uk_ref[...], uv_ref[...], keys_ref[0]
    rows = q.shape[0]
    halves = (0, HEAD)
    scores = pair_scores(ql, keys, qpos_ref[0], kpos_ref[0])
    probs = jnp.exp(scores - lse_ref[0, 0])
    dmixed = jnp.concatenate(
        [times_transposed(dval[:, k : k + HEAD], uv[:, k : k + HEAD]) for k in halves], 0
    ).astype(BF16)
    dprobs = times_transposed(dmixed, keys)
    dscores = probs * (dprobs - jnp.sum(probs * dprobs, -1, keepdims=True))
    dscores = dscores.astype(BF16) * jnp.asarray(SCALE, BF16)
    dql = product(dscores, keys).astype(BF16)
    dkeys = contract_rows(dscores, ql) + contract_rows(probs.astype(BF16), dmixed)

    @pl.when(pair == 0)
    def _():
        keys_acc[...] = dkeys

    @pl.when(pair > 0)
    def _():
        keys_acc[...] += dkeys

    guk = jnp.concatenate(
        [contract_rows(dql[n * rows : (n + 1) * rows], q[:, k : k + HEAD]) for n, k in enumerate(halves)], 1
    )
    guv = jnp.concatenate(
        [contract_rows(mixed[n * rows : (n + 1) * rows], dval[:, k : k + HEAD]) for n, k in enumerate(halves)], 1
    )

    @pl.when(seq == 0)
    def _():
        uk_acc[pair] = guk
        uv_acc[pair] = guv

    @pl.when(seq > 0)
    def _():
        uk_acc[pair] += guk
        uv_acc[pair] += guv

    dq_ref[0] = jnp.concatenate(
        [product(dql[n * rows : (n + 1) * rows], uk[:, k : k + HEAD]) for n, k in enumerate(halves)], 1
    ).astype(BF16)
    last = pl.num_programs(1) - 1

    @pl.when(pair == last)
    def _():
        count = dkeys_refs[0].shape[0]
        for n, ref in enumerate(dkeys_refs):
            part = keys_acc[n * count * rows : (n + 1) * count * rows, :]
            ref[:, 0] = part.reshape(count, rows, LATENT).astype(BF16)

    @pl.when((pair == last) & (seq == pl.num_programs(0) - 1))
    def _():
        for n in range(uk_acc.shape[0]):
            guk_ref[:, 2 * n * HEAD : 2 * (n + 1) * HEAD] = uk_acc[n].astype(BF16)
            guv_ref[:, 2 * n * HEAD : 2 * (n + 1) * HEAD] = uv_acc[n].astype(BF16)


def attention_specs(length, rows):
    pair = pl.BlockSpec((1, rows, 2 * HEAD), lambda s, p: (s, 0, p))
    up = pl.BlockSpec((LATENT, 2 * HEAD), lambda s, p: (0, p))
    keys = pl.BlockSpec((1, length, LATENT), lambda s, p: (s, 0, 0))
    query_pos = pl.BlockSpec((1, rows, 1), lambda s, p: (s, 0, 0))
    key_pos = pl.BlockSpec((1, 1, length), lambda s, p: (s, 0, 0))
    wide = pl.BlockSpec((1, 1, 2 * rows, LATENT), lambda s, p: (s, p, 0, 0))
    thin = pl.BlockSpec((1, 1, 2 * rows, 1), lambda s, p: (s, p, 0, 0))
    return pair, up, keys, query_pos, key_pos, wide, thin


def attend(q, uk, uv, keys, query_pos, key_pos):
    seqs, length, _ = keys.shape
    rows, pairs = q.shape[1], q.shape[2] // (2 * HEAD)
    pair, up, key, qpos, kpos, wide, thin = attention_specs(length, rows)
    flops = seqs * pairs * 2 * rows * length * LATENT * 4
    return pl.pallas_call(
        attend_kernel,
        grid=(seqs, pairs),
        in_specs=[pair, up, up, key, qpos, kpos],
        out_specs=[wide, wide, thin, pair],
        out_shape=[
            jax.ShapeDtypeStruct((seqs, pairs, 2 * rows, LATENT), BF16),
            jax.ShapeDtypeStruct((seqs, pairs, 2 * rows, LATENT), BF16),
            jax.ShapeDtypeStruct((seqs, pairs, 2 * rows, 1), F32),
            jax.ShapeDtypeStruct(q.shape, BF16),
        ],
        compiler_params=pltpu.CompilerParams(vmem_limit_bytes=VMEM_BYTES),
        cost_estimate=pl.CostEstimate(flops=flops, bytes_accessed=6 << 20, transcendentals=seqs * pairs * 2 * rows * length),
        name="attend",
    )(q, uk, uv, keys, query_pos, key_pos)


def attend_back(q, ql, mixed, lse, dval, uk, uv, keys, query_pos, key_pos, parts):
    seqs, length, _ = keys.shape
    rows, pairs = q.shape[1], q.shape[2] // (2 * HEAD)
    pair, up, key, qpos, kpos, wide, thin = attention_specs(length, rows)
    whole = pl.BlockSpec(uk.shape, lambda s, p: (0, 0))
    count = length // rows // parts
    flops = seqs * pairs * 2 * rows * length * LATENT * 10
    return pl.pallas_call(
        attend_back_kernel,
        grid=(seqs, pairs),
        in_specs=[pair, wide, wide, thin, pair, up, up, key, qpos, kpos],
        out_specs=[pair, whole, whole]
        + [pl.BlockSpec((count, 1, rows, LATENT), lambda s, p: (0, s, 0, 0))] * parts,
        out_shape=[jax.ShapeDtypeStruct(q.shape, BF16)]
        + [jax.ShapeDtypeStruct(uk.shape, BF16)] * 2
        + [jax.ShapeDtypeStruct((count, seqs, rows, LATENT), BF16)] * parts,
        scratch_shapes=[
            pltpu.VMEM((length, LATENT), F32),
            pltpu.VMEM((pairs, LATENT, 2 * HEAD), F32),
            pltpu.VMEM((pairs, LATENT, 2 * HEAD), F32),
        ],
        compiler_params=pltpu.CompilerParams(vmem_limit_bytes=VMEM_BYTES),
        cost_estimate=pl.CostEstimate(flops=flops, bytes_accessed=8 << 20, transcendentals=seqs * pairs * 2 * rows * length),
        name="attend_back",
    )(q, ql, mixed, lse, dval, uk, uv, keys, query_pos, key_pos)


class Plan:
    def __init__(self, mesh):
        self.dp, self.ctx = mesh.shape["dp"], mesh.shape["ctx"]
        self.count = self.dp * self.ctx
        self.core = self.ctx
        self.cross = 2 * self.ctx
        top = self.count // 2
        bits = [1 << n for n in range(self.count.bit_length() - 1)]
        ctx_bits = [b for b in bits if b < self.ctx]
        self.half_bits = [b for b in bits if b != self.core]
        self.split_bits = [self.core, self.cross]
        self.quarter_bits = [b for b in bits if b not in self.split_bits]
        self.ctx_bits = ctx_bits
        self.top = top

    def swap(self, value, mask):
        return lax.ppermute(value, AXES, [(n, n ^ mask) for n in range(self.count)])

    def swap_bits(self, number, first, second):
        if first == second:
            return number
        one, two = (number // first) % 2, (number // second) % 2
        return number + (two - one) * first + (one - two) * second

    def deal(self, value, pairs):
        table = []
        for n in range(self.count):
            m = n
            for first, second in pairs:
                m = self.swap_bits(m, first, second)
            table.append((n, m))
        if all(a == b for a, b in table):
            return value
        return lax.ppermute(value, AXES, table)


def masks_of(bits):
    out = [0]
    for bit in bits:
        out = out + [m ^ bit for m in out]
    return out


def gather(plan, value, far, bits, groups):
    done = [([m], value[None] if m == 0 else plan.swap(value, m)[None]) for m in masks_of(far)]
    for bit, count in zip(bits, groups):
        size = -(-len(done) // count)
        sent = []
        for at in range(0, len(done), size):
            some = done[at : at + size]
            masks = [m for ms, _ in some for m in ms]
            stack = some[0][1] if len(some) == 1 else jnp.concatenate([a for _, a in some])
            sent.append(([m ^ bit for m in masks], plan.swap(stack, bit)))
        done = done + sent
    return done


def reduce_order(far, second, first):
    base = masks_of(far)
    return [[m ^ one ^ two for m in base] for one in (0, first) for two in (0, second)]


def reduce_far(plan, part, far):
    total = part[0].astype(F32)
    for n, mask in enumerate(masks_of(far)):
        if n:
            total = total + plan.swap(part[n].astype(BF16), mask).astype(F32)
    return total


def reduce(plan, stacks, far, second, first):
    keep0, keep1, send0, send1 = stacks
    got1 = plan.swap(send1, first)
    got0 = plan.swap(send0, first)
    part1 = (keep1.astype(F32) + got1.astype(F32)).astype(BF16)
    got = plan.swap(part1, second)
    return reduce_far(plan, (keep0.astype(F32) + got0.astype(F32) + got.astype(F32)).astype(BF16), far)


def per_device(plan, tokens, cotangent, domain_ids, domain_weights, stretch_offsets, gain_attn, gain_ffn,
               w_query, w_latent, w_upkey, w_upvalue, w_out, w_gate, w_up, w_down):
    _, rows, width = tokens.shape
    me = lax.axis_index("dp") * plan.ctx + lax.axis_index("ctx")
    here = lax.axis_index("ctx")
    core = (me // plan.core) % 2
    core_bit, cross_bit = plan.core, plan.cross
    count = plan.count
    shard = w_query.shape[0]
    up_shard = w_upkey.shape[0]
    down_shard = w_down.shape[0]
    half = w_query.shape[1] // 2
    latent_half = w_latent.shape[1] // 2
    pair_width = w_upkey.shape[1]
    quarter = w_gate.shape[1] // 4
    y_bit, *z_bits = plan.ctx_bits
    x_bit = plan.half_bits[-1]
    half_far = [b for b in plan.half_bits if b not in (x_bit, y_bit)]
    extra_bits = [b for b in plan.quarter_bits if b not in plan.ctx_bits]
    half_stages = (half_far, y_bit, x_bit)

    def halves(value, size):
        low, high = value[:, :size], value[:, size:]
        return jnp.where(core == 0, low, high), jnp.where(core == 0, high, low)

    query_own, query_other = halves(w_query, half)
    latent_own, latent_other = halves(w_latent, latent_half)
    info = jnp.concatenate([gain_attn, gain_ffn, stretch_offsets[0].astype(BF16)])
    info = jnp.pad(info[None], ((0, INFO - 1), (0, latent_half - info.shape[0])))
    band = shard + INFO
    folds = half // latent_half
    fold = lambda value: jnp.concatenate(jnp.split(value, folds, 1), 0)
    unfold = lambda value: jnp.concatenate(jnp.split(value, folds, 0), 1)
    got = plan.swap(jnp.concatenate([latent_other, info, fold(query_other)]), core_bit)
    first_message = jnp.concatenate([latent_own, info, got[:band]])
    dealt = plan.deal(
        jnp.concatenate([jnp.concatenate([w_upkey, w_upvalue], 1), w_out]), [(plan.top, core_bit)]
    )
    second_message = jnp.concatenate([jnp.concatenate([query_own, unfold(got[band:])], 1), dealt])
    split_masks = masks_of(plan.split_bits)
    split = (me // core_bit) % 2 + 2 * ((me // cross_bit) % 2)
    columns = jnp.concatenate([w_gate, w_up]).reshape(2 * shard, 4, quarter).transpose(1, 0, 2)

    def quarter_of(mask_index):
        return lax.dynamic_index_in_dim(columns, split ^ mask_index, 0, keepdims=False)

    down = plan.deal(w_down, [(plan.top, cross_bit), (plan.top // 2, core_bit)])
    low_width = min(quarter // 128 * 128, width)
    down_widths = [low_width, width - low_width]

    def narrow(value, column, columns):
        return jnp.pad(value[:, column : column + columns], ((0, 0), (0, quarter - columns)))

    third_message = jnp.concatenate(
        [quarter_of(0)]
        + [plan.swap(quarter_of(n), m) for n, m in enumerate(split_masks) if n]
        + [narrow(down, column, columns) for columns, column in bands_of(down_widths)]
    )
    columns_rows = 8 * shard
    third_rows = third_message.shape[0]

    tokens_two = jnp.concatenate([tokens[0], plan.swap(tokens[0], core_bit)])
    x_two = tokens_two.astype(F32)

    first_pieces = gather(plan, first_message, half_far, (y_bit, x_bit), (1, 1))
    second_pieces = gather(plan, second_message, half_far, (y_bit, x_bit), (4, 2))
    third_stack = jnp.concatenate([a for _, a in gather(plan, third_message, extra_bits, (), ())])
    extra_masks = masks_of(extra_bits)
    third_whole = lax.all_gather(third_stack, "ctx", axis=0, tiled=True)
    third_spots = [(c * len(extra_masks) + e, (me - here + c) ^ m) for c in range(plan.ctx) for e, m in enumerate(extra_masks)]

    def spots(pieces):
        return [(i, j, m) for i, (masks, _) in enumerate(pieces) for j, m in enumerate(masks)]

    def owner_half(number):
        return plan.swap_bits(number, plan.top, core_bit) % (count // 2)

    def owner_quarter(number):
        source = plan.swap_bits(number, plan.top // 2, core_bit)
        return plan.swap_bits(source, plan.top, cross_bit) % (count // 4)

    found = spots(first_pieces)
    (latent_full,) = place_blocks(
        [a for _, a in first_pieces],
        [[[(i, j, b * band, 0) for i, j, _ in found for b in (0, 1)]]],
        [[me ^ (m ^ b * core_bit) for _, _, m in found for b in (0, 1)]],
        [(shard, [latent_half])],
    )
    rows_info = jnp.concatenate(
        [a[:, shard :: band, : 2 * shard + 1] for _, a in first_pieces]
    )

    found = spots(second_pieces)
    owners = [owner_half(me ^ m) for _, _, m in found]
    query_full, upkey_full, upvalue_full, out_full = place_blocks(
        [a for _, a in second_pieces],
        [
            [[(i, j, 0, b * half) for i, j, _ in found for b in (0, 1)]],
            [[(i, j, shard, 0) for i, j, _ in found]],
            [[(i, j, shard, pair_width) for i, j, _ in found]],
            [[(i, j, shard + up_shard, 0) for i, j, _ in found]],
        ],
        [[me ^ (m ^ b * core_bit) for _, _, m in found for b in (0, 1)], owners, owners, owners],
        [(shard, [half]), (up_shard, [pair_width]), (up_shard, [pair_width]), (shard, [width])],
    )

    column_order = [number ^ s for _, number in third_spots for s in split_masks]
    down_order = [owner_quarter(number) for _, number in third_spots]
    third_blocks = [
        [[(0, j, n * 2 * shard, 0) for j, _ in third_spots for n in range(4)]],
        [[(0, j, n * 2 * shard + shard, 0) for j, _ in third_spots for n in range(4)]],
        [[(0, j, columns_rows + n * down_shard, 0) for j, _ in third_spots] for n in (0, 1)],
    ]
    third_orders = [column_order, column_order, down_order]
    third_shapes = [(shard, [quarter]), (shard, [quarter]), (down_shard, down_widths)]
    gate_full, up_full, down_full = place_blocks([third_whole], third_blocks, third_orders, third_shapes)

    masks_info = [m for _, _, m in spots(first_pieces)]
    number = jnp.stack([jnp.stack([me ^ m, me ^ m ^ core_bit]) for m in masks_info]).reshape(-1)
    chosen = (number[:, None] == jnp.arange(count)[None, :]).astype(BF16)
    gains = contract_rows(chosen, rows_info[..., : 2 * shard].reshape(count, 2 * shard))
    gain_one = gains[:, :shard].reshape(width)
    gain_two = gains[:, shard:].reshape(width)
    ctx_masks = [m ^ y for y in (0, y_bit) for m in masks_of(z_bits)]
    offsets = jnp.stack(
        [rows_info[masks_info.index(m), :, 2 * shard] for m in ctx_masks], 1
    ).astype(jnp.int32)
    within = jnp.arange(rows, dtype=jnp.int32)
    key_pos = (offsets[:, :, None] * rows + within).reshape(2, 1, -1)
    query_pos = (offsets[:, :1] * rows + within)[:, :, None]

    normed_one = (x_two * inverse_rms(x_two) * gain_one).astype(BF16)
    latent = product(normed_one, latent_full).astype(BF16)
    latent_message = latent.reshape(2, rows, latent_half)
    key_pieces = gather(plan, latent_message, z_bits, (y_bit,), (4,))
    key_of = {m: a[j] for masks, a in key_pieces for j, m in enumerate(masks)}
    keys = jnp.concatenate([key_of[m] for m in ctx_masks], 1)
    queries = product(normed_one, query_full).astype(BF16).reshape(2, rows, half)
    query_latent, mixed, lse, values = attend(queries, upkey_full, upvalue_full, keys, query_pos, key_pos)
    values = values.reshape(2 * rows, half)
    shares = product(values, out_full)
    x_own = x_two[:rows]
    middle = x_own + shares[:rows] + plan.swap(shares[rows:], core_bit)

    def spread(value):
        near = plan.swap(value, core_bit)
        across = plan.swap(value, cross_bit)
        return jnp.concatenate([value, near, across, plan.swap(across, core_bit)])

    def collect(shares):
        parts = shares.reshape(4, rows, width)
        got = plan.swap(jnp.stack([parts[1], parts[3]]), core_bit)
        across = plan.swap((parts[2] + got[1]).astype(BF16), cross_bit)
        return parts[0] + got[0] + across.astype(F32)

    match = domain_ids[:, None] == jnp.arange(DOMAINS, dtype=jnp.int32)[None, :]
    scale = jnp.sum(jnp.where(match, domain_weights[None, :], 0.0))
    dlayer = cotangent[0].astype(F32) * scale
    dy = spread(dlayer.astype(BF16))

    normed_two = spread((middle * inverse_rms(middle) * gain_two).astype(BF16))
    gate = product(normed_two, gate_full)
    up = product(normed_two, up_full)
    sigmoid = jax.nn.sigmoid(gate)
    silu = gate * sigmoid
    hidden = (silu * up).astype(BF16)
    dhidden = times_transposed(dy, down_full)
    dgate = (dhidden * up * (sigmoid * (1.0 + gate * (1.0 - sigmoid)))).astype(BF16)
    dup = (dhidden * silu).astype(BF16)
    dnormed_two = collect(times_transposed(dgate, gate_full) + times_transposed(dup, up_full))
    grad_gate = contract_rows(normed_two, dgate).astype(BF16)
    grad_up = contract_rows(normed_two, dup).astype(BF16)
    grad_down = contract_rows(hidden, dy).astype(BF16)
    output = (middle + collect(product(hidden, down_full))).astype(BF16)[None]

    (third_grads,) = cut_blocks(
        [grad_gate, grad_up, grad_down], third_blocks, third_orders, third_shapes,
        [(len(third_spots), third_rows, quarter)],
        [(0, columns_rows + n * down_shard, down_shard, w, quarter - w) for n, w in enumerate(down_widths) if w < quarter],
    )
    third_sum = reduce_far(
        plan, lax.psum_scatter(third_grads, "ctx", scatter_dimension=0, tiled=True), extra_bits
    )
    down_sum = third_sum[columns_rows:].reshape(2, down_shard, quarter)
    down_sum = jnp.concatenate([down_sum[n, :, :w] for n, w in enumerate(down_widths)], 1)
    grad_w_down = plan.deal(down_sum, [(plan.top // 2, core_bit), (plan.top, cross_bit)])
    column_sum = third_sum[:columns_rows].reshape(4, 2 * shard, quarter)
    got = [column_sum[0]] + [
        plan.swap(column_sum[n].astype(BF16), m).astype(F32) for n, m in enumerate(split_masks) if n
    ]
    got = jnp.stack(got)
    grad_columns = jnp.concatenate(
        [lax.dynamic_index_in_dim(got, split ^ n, 0, keepdims=False) for n in range(4)], 1
    )
    grad_w_gate, grad_w_up = grad_columns[:shard], grad_columns[shard:]

    dmiddle_norm, grad_gain_two = norm_back(middle, gain_two, dnormed_two)
    dmiddle = dlayer + dmiddle_norm
    dm = dmiddle.astype(BF16)
    dm_two = jnp.concatenate([dm, plan.swap(dm, core_bit)])
    grad_out = contract_rows(values, dm_two).astype(BF16)
    dvalues = times_transposed(dm_two, out_full).astype(BF16).reshape(2, rows, half)
    dqueries, grad_upkey, grad_upvalue, keep, send = attend_back(
        queries, query_latent, mixed, lse, dvalues, upkey_full, upvalue_full, keys, query_pos, key_pos, 2
    )
    dlatent = reduce_far(plan, keep.astype(F32) + plan.swap(send, y_bit).astype(F32), z_bits)
    dlatent = dlatent.astype(BF16).reshape(2 * rows, latent_half)
    dqueries = dqueries.reshape(2 * rows, half)
    shares = times_transposed(dqueries, query_full) + times_transposed(dlatent, latent_full)
    dnormed_one = shares[:rows] + plan.swap(shares[rows:], core_bit)
    dx_norm, grad_gain_one = norm_back(x_own, gain_one, dnormed_one)
    grad_tokens = (dmiddle + dx_norm).astype(BF16)[None]

    half_order = reduce_order(*half_stages)
    places = [(i, j, m) for i, masks in enumerate(half_order) for j, m in enumerate(masks)]
    owners = [owner_half(me ^ m) for _, _, m in places]
    grad_query = contract_rows(normed_one, dqueries).astype(BF16)
    second_stacks = cut_blocks(
        [grad_query, grad_upkey, grad_upvalue, grad_out],
        [
            [[(i, j, 0, b * half) for i, j, _ in places for b in (0, 1)]],
            [[(i, j, shard, 0) for i, j, _ in places]],
            [[(i, j, shard, pair_width) for i, j, _ in places]],
            [[(i, j, shard + up_shard, 0) for i, j, _ in places]],
        ],
        [[me ^ (m ^ b * core_bit) for _, _, m in places for b in (0, 1)], owners, owners, owners],
        [(shard, [half]), (up_shard, [pair_width]), (up_shard, [pair_width]), (shard, [width])],
        [(len(masks),) + second_message.shape for masks in half_order],
    )
    second_sum = reduce(plan, second_stacks, *half_stages)
    own, got = second_sum[:shard, :half], plan.swap(second_sum[:shard, half:].astype(BF16), core_bit).astype(F32)
    grad_w_query = jnp.concatenate([jnp.where(core == 0, own, got), jnp.where(core == 0, got, own)], 1)
    dealt = plan.deal(second_sum[shard:].astype(BF16), [(plan.top, core_bit)]).astype(F32)
    grad_w_out = dealt[up_shard:]

    grad_latent = contract_rows(normed_one, dlatent).astype(BF16)
    gain_rows = jnp.concatenate([grad_gain_one.reshape(count, shard), grad_gain_two.reshape(count, shard)], 1)
    gain_rows = jnp.pad(gain_rows.astype(BF16)[:, None], ((0, 0), (0, INFO - 1), (0, latent_half - 2 * shard)))
    order = [me ^ (m ^ b * core_bit) for _, _, m in places for b in (0, 1)]
    first_stacks = cut_blocks(
        [grad_latent, gain_rows.reshape(count * INFO, latent_half)],
        [
            [[(i, j, b * band, 0) for i, j, _ in places for b in (0, 1)]],
            [[(i, j, b * band + shard, 0) for i, j, _ in places for b in (0, 1)]],
        ],
        [order, order],
        [(shard, [latent_half]), (INFO, [latent_half])],
        [(len(masks), 2 * band, latent_half) for masks in half_order],
    )
    first_sum = reduce(plan, first_stacks, *half_stages)
    own, got = first_sum[:band], plan.swap(first_sum[band:].astype(BF16), core_bit).astype(F32)
    grad_w_latent = jnp.concatenate([jnp.where(core == 0, own, got), jnp.where(core == 0, got, own)], 1)[:shard]
    gain_sums = own[shard] + got[shard]

    return (
        output, grad_tokens, gain_sums[:shard], gain_sums[shard : 2 * shard],
        grad_w_query, grad_w_latent, dealt[:up_shard, :pair_width], dealt[:up_shard, pair_width:],
        grad_w_out, grad_w_gate, grad_w_up, grad_w_down,
    )


def solution(mesh):
    rows = P(("dp", "ctx"), None)
    vector = P(("dp", "ctx"))
    stretch = P("dp", "ctx", None)
    in_specs = (stretch, stretch, P("dp"), P(), P("dp", "ctx"), vector, vector) + (rows,) * 8
    out_specs = (stretch, stretch, vector, vector) + (rows,) * 8
    return jax.shard_map(
        functools.partial(per_device, Plan(mesh)), mesh=mesh, in_specs=in_specs, out_specs=out_specs,
        check_vma=False,
    )
```

```python
import functools
import itertools
import math

import jax
import jax.numpy as jnp
from jax import lax
from jax.experimental import pallas as pl
from jax.experimental.pallas import tpu as pltpu
from jax.sharding import PartitionSpec as P

PAIRS_A_STEP = 2
HEAD = 64
LATENT = 256
DOMAINS = 8
EPS = 1e-06
SCALE = 0.125
MASKED = -1e30
AXES = ("dp", "ctx")
BF16 = jnp.bfloat16
F32 = jnp.float32
INFO = 8
VMEM_BYTES = 56 * 1024 * 1024


def product(left, right):
    return jnp.dot(left, right, preferred_element_type=F32)


def contract_rows(left, right):
    return lax.dot_general(left, right, (((0,), (0,)), ((), ())), preferred_element_type=F32)


def times_transposed(left, right):
    return lax.dot_general(left, right, (((1,), (1,)), ((), ())), preferred_element_type=F32)


def inverse_rms(rows):
    return lax.rsqrt(jnp.mean(rows * rows, -1, keepdims=True) + EPS)


def norm_back(rows, gain, grad):
    r = inverse_rms(rows)
    grad_gain = jnp.sum(grad * rows * r, 0)
    scaled = grad * gain
    mean = jnp.mean(scaled * rows, -1, keepdims=True)
    return r * scaled - rows * (r * r * r * mean), grad_gain


def groups_of(spots):
    groups = {}
    for n, (i, j, r, k) in enumerate(spots):
        groups.setdefault((i, r, k), []).append((j, n))
    return [(key, [n for _, n in sorted(found)]) for key, found in groups.items()]


def permute_blocks(chosen, stack):
    out = product(chosen.astype(BF16), stack.reshape(stack.shape[0], -1)).astype(BF16)
    return out.reshape(-1, *stack.shape[1:])


def bands_of(widths):
    return list(zip(widths, itertools.accumulate([0, *widths[:-1]])))


def kernel_bytes(shapes):
    return 4 * sum(math.prod(shape) for shape in shapes) + (4 << 20)


def place_blocks(pieces, blocks, orders, shapes):
    if any(rows % 8 for rows, _ in shapes):
        made = []
        for (rows, widths), bands, order in zip(shapes, blocks, orders):
            parts = []
            for (width, _), spots in zip(bands_of(widths), bands):
                groups = groups_of(spots)
                stack = jnp.concatenate([pieces[i][:, r : r + rows, k : k + width] for (i, r, k), _ in groups])
                own = jnp.stack([order[n] for _, ns in groups for n in ns])
                numbers = jnp.arange(len(spots), dtype=own.dtype)
                parts.append(permute_blocks(own[None, :] == numbers[:, None], stack))
            made.append(jnp.concatenate(parts, 2).reshape(-1, sum(widths)))
        return made

    def kernel(order_ref, *refs):
        sources, targets = refs[: len(pieces)], refs[len(pieces) :]
        first = 0
        for target, (rows, widths), bands in zip(targets, shapes, blocks):
            for (width, column), spots in zip(bands_of(widths), bands):
                for n, (i, j, r, k) in enumerate(spots):
                    target[order_ref[first + n], :, column : column + width] = sources[i][
                        j, r : r + rows, k : k + width
                    ]
            first += len(bands[0])

    out_shapes = [(len(bands[0]), rows, sum(widths)) for (rows, widths), bands in zip(shapes, blocks)]
    made = pl.pallas_call(
        kernel,
        out_shape=[jax.ShapeDtypeStruct(shape, BF16) for shape in out_shapes],
        in_specs=[pl.BlockSpec(memory_space=pltpu.SMEM)]
        + [pl.BlockSpec(memory_space=pltpu.VMEM)] * len(pieces),
        out_specs=[pl.BlockSpec(memory_space=pltpu.VMEM)] * len(shapes),
        compiler_params=pltpu.CompilerParams(
            vmem_limit_bytes=kernel_bytes(out_shapes + [p.shape for p in pieces])
        ),
        name="place_blocks",
    )(jnp.stack([n for order in orders for n in order]), *pieces)
    return [whole.reshape(-1, whole.shape[-1]) for whole in made]


def cut_blocks(matrices, blocks, orders, shapes, piece_shapes, spare=()):
    if any(rows % 8 for rows, _ in shapes):
        bands_at = [{} for _ in piece_shapes]
        for (rows, widths), bands, order, matrix in zip(shapes, blocks, orders, matrices):
            grid = matrix.reshape(len(bands[0]), rows, -1)
            for (width, column), spots in zip(bands_of(widths), bands):
                for (i, r, k), ns in groups_of(spots):
                    own = jnp.stack([order[n] for n in ns])
                    chosen = own[:, None] == jnp.arange(len(spots), dtype=own.dtype)[None, :]
                    bands_at[i].setdefault(r, {})[k] = permute_blocks(chosen, grid[:, :, column : column + width])
        for i, r, rows, k, columns in spare:
            bands_at[i].setdefault(r, {})[k] = jnp.zeros((piece_shapes[i][0], rows, columns), BF16)
        return [
            jnp.concatenate(
                [jnp.concatenate([row[k] for k in sorted(row)], 2) for _, row in sorted(band.items())], 1
            )
            for band in bands_at
        ]

    def kernel(order_ref, *refs):
        sources, targets = refs[: len(matrices)], refs[len(matrices) :]
        for i, r, rows, k, columns in spare:
            targets[i][:, r : r + rows, k : k + columns] = jnp.zeros((piece_shapes[i][0], rows, columns), BF16)
        first = 0
        for source, (rows, widths), bands in zip(sources, shapes, blocks):
            for (width, column), spots in zip(bands_of(widths), bands):
                for n, (i, j, r, k) in enumerate(spots):
                    targets[i][j, r : r + rows, k : k + width] = source[
                        order_ref[first + n], :, column : column + width
                    ]
            first += len(bands[0])

    grids = [matrix.reshape(-1, rows, matrix.shape[-1]) for matrix, (rows, _) in zip(matrices, shapes)]
    return pl.pallas_call(
        kernel,
        out_shape=[jax.ShapeDtypeStruct(shape, BF16) for shape in piece_shapes],
        in_specs=[pl.BlockSpec(memory_space=pltpu.SMEM)]
        + [pl.BlockSpec(memory_space=pltpu.VMEM)] * len(matrices),
        out_specs=[pl.BlockSpec(memory_space=pltpu.VMEM)] * len(piece_shapes),
        compiler_params=pltpu.CompilerParams(
            vmem_limit_bytes=kernel_bytes(list(piece_shapes) + [g.shape for g in grids])
        ),
        name="cut_blocks",
    )(jnp.stack([n for order in orders for n in order]), *grids)


def pair_scores(query_latent, keys, visible):
    scores = times_transposed(query_latent * jnp.asarray(SCALE, BF16), keys)
    return jnp.where(visible, scores, MASKED)


def visible_keys(query_pos, key_pos):
    return jnp.concatenate([query_pos, query_pos], 0) >= key_pos


def pair_lanes(n):
    return slice(2 * n * HEAD, 2 * (n + 1) * HEAD)


def attend_kernel(q_ref, uk_ref, uv_ref, keys_ref, qpos_ref, kpos_ref, ql_ref, mixed_ref, lse_ref, values_ref):
    keys = keys_ref[0]
    visible = visible_keys(qpos_ref[0], kpos_ref[0])
    for n in range(ql_ref.shape[1]):
        lanes = pair_lanes(n)
        q, uk, uv = q_ref[0][:, lanes], uk_ref[:, lanes], uv_ref[:, lanes]
        rows = q.shape[0]
        ql = jnp.concatenate(
            [times_transposed(q[:, k : k + HEAD], uk[:, k : k + HEAD]) for k in (0, HEAD)], 0
        ).astype(BF16)
        scores = pair_scores(ql, keys, visible)
        top = jnp.max(scores, -1, keepdims=True)
        terms = jnp.exp(scores - top)
        total = jnp.sum(terms, -1, keepdims=True)
        probs = (terms * (1.0 / total)).astype(BF16)
        mixed = product(probs, keys).astype(BF16)
        ql_ref[0, n] = ql
        mixed_ref[0, n] = mixed
        lse_ref[0, n] = top + jnp.log(total)
        values_ref[0, :, lanes] = jnp.concatenate(
            [product(mixed[:rows], uv[:, :HEAD]), product(mixed[rows:], uv[:, HEAD:])], 1
        ).astype(BF16)


def attend_back_kernel(
    q_ref, ql_ref, mixed_ref, lse_ref, dval_ref, uk_ref, uv_ref, keys_ref, qpos_ref, kpos_ref,
    dq_ref, guk_ref, guv_ref, *rest,
):
    dkeys_refs, (keys_acc, uk_acc, uv_acc) = rest[:-3], rest[-3:]
    seq, step = pl.program_id(0), pl.program_id(1)
    keys = keys_ref[0]
    visible = visible_keys(qpos_ref[0], kpos_ref[0])
    halves = (0, HEAD)
    inside = ql_ref.shape[1]
    dkeys = None
    for n in range(inside):
        lanes = pair_lanes(n)
        q, dval, uk, uv = q_ref[0][:, lanes], dval_ref[0][:, lanes], uk_ref[:, lanes], uv_ref[:, lanes]
        ql, mixed = ql_ref[0, n], mixed_ref[0, n]
        rows = q.shape[0]
        scores = pair_scores(ql, keys, visible)
        probs = jnp.exp(scores - lse_ref[0, n])
        dmixed = jnp.concatenate(
            [times_transposed(dval[:, k : k + HEAD], uv[:, k : k + HEAD]) for k in halves], 0
        ).astype(BF16)
        dprobs = times_transposed(dmixed, keys)
        dscores = probs * (dprobs - jnp.sum(probs * dprobs, -1, keepdims=True))
        dscores = dscores.astype(BF16) * jnp.asarray(SCALE, BF16)
        dql = product(dscores, keys).astype(BF16)
        part = contract_rows(dscores, ql) + contract_rows(probs.astype(BF16), dmixed)
        dkeys = part if dkeys is None else dkeys + part
        guk = jnp.concatenate(
            [contract_rows(dql[i * rows : (i + 1) * rows], q[:, k : k + HEAD]) for i, k in enumerate(halves)], 1
        )
        guv = jnp.concatenate(
            [contract_rows(mixed[i * rows : (i + 1) * rows], dval[:, k : k + HEAD]) for i, k in enumerate(halves)], 1
        )
        pair = step * inside + n
        uk_acc[pair] = jnp.where(seq == 0, guk, uk_acc[pair] + guk)
        uv_acc[pair] = jnp.where(seq == 0, guv, uv_acc[pair] + guv)
        dq_ref[0, :, lanes] = jnp.concatenate(
            [product(dql[i * rows : (i + 1) * rows], uk[:, k : k + HEAD]) for i, k in enumerate(halves)], 1
        ).astype(BF16)

    @pl.when(step == 0)
    def _():
        keys_acc[...] = dkeys

    @pl.when(step > 0)
    def _():
        keys_acc[...] += dkeys

    last = pl.num_programs(1) - 1

    @pl.when(step == last)
    def _():
        count = dkeys_refs[0].shape[0]
        for n, ref in enumerate(dkeys_refs):
            part = keys_acc[n * count * rows : (n + 1) * count * rows, :]
            ref[:, 0] = part.reshape(count, rows, LATENT).astype(BF16)

    @pl.when((step == last) & (seq == pl.num_programs(0) - 1))
    def _():
        for n in range(uk_acc.shape[0]):
            guk_ref[:, pair_lanes(n)] = uk_acc[n].astype(BF16)
            guv_ref[:, pair_lanes(n)] = uv_acc[n].astype(BF16)


def attention_specs(length, rows):
    pair = pl.BlockSpec((1, rows, 2 * PAIRS_A_STEP * HEAD), lambda s, p: (s, 0, p))
    up = pl.BlockSpec((LATENT, 2 * PAIRS_A_STEP * HEAD), lambda s, p: (0, p))
    keys = pl.BlockSpec((1, length, LATENT), lambda s, p: (s, 0, 0))
    query_pos = pl.BlockSpec((1, rows, 1), lambda s, p: (s, 0, 0))
    key_pos = pl.BlockSpec((1, 1, length), lambda s, p: (s, 0, 0))
    wide = pl.BlockSpec((1, PAIRS_A_STEP, 2 * rows, LATENT), lambda s, p: (s, p, 0, 0))
    thin = pl.BlockSpec((1, PAIRS_A_STEP, 2 * rows, 1), lambda s, p: (s, p, 0, 0))
    return pair, up, keys, query_pos, key_pos, wide, thin


def attend(q, uk, uv, keys, query_pos, key_pos):
    seqs, length, _ = keys.shape
    rows, pairs = q.shape[1], q.shape[2] // (2 * HEAD)
    pair, up, key, qpos, kpos, wide, thin = attention_specs(length, rows)
    flops = seqs * pairs * 2 * rows * length * LATENT * 4
    return pl.pallas_call(
        attend_kernel,
        grid=(seqs, pairs // PAIRS_A_STEP),
        in_specs=[pair, up, up, key, qpos, kpos],
        out_specs=[wide, wide, thin, pair],
        out_shape=[
            jax.ShapeDtypeStruct((seqs, pairs, 2 * rows, LATENT), BF16),
            jax.ShapeDtypeStruct((seqs, pairs, 2 * rows, LATENT), BF16),
            jax.ShapeDtypeStruct((seqs, pairs, 2 * rows, 1), F32),
            jax.ShapeDtypeStruct(q.shape, BF16),
        ],
        compiler_params=pltpu.CompilerParams(vmem_limit_bytes=VMEM_BYTES),
        cost_estimate=pl.CostEstimate(flops=flops, bytes_accessed=6 << 20, transcendentals=seqs * pairs * 2 * rows * length),
        name="attend",
    )(q, uk, uv, keys, query_pos, key_pos)


def attend_back(q, ql, mixed, lse, dval, uk, uv, keys, query_pos, key_pos, parts):
    seqs, length, _ = keys.shape
    rows, pairs = q.shape[1], q.shape[2] // (2 * HEAD)
    pair, up, key, qpos, kpos, wide, thin = attention_specs(length, rows)
    whole = pl.BlockSpec(uk.shape, lambda s, p: (0, 0))
    count = length // rows // parts
    flops = seqs * pairs * 2 * rows * length * LATENT * 10
    return pl.pallas_call(
        attend_back_kernel,
        grid=(seqs, pairs // PAIRS_A_STEP),
        in_specs=[pair, wide, wide, thin, pair, up, up, key, qpos, kpos],
        out_specs=[pair, whole, whole]
        + [pl.BlockSpec((count, 1, rows, LATENT), lambda s, p: (0, s, 0, 0))] * parts,
        out_shape=[jax.ShapeDtypeStruct(q.shape, BF16)]
        + [jax.ShapeDtypeStruct(uk.shape, BF16)] * 2
        + [jax.ShapeDtypeStruct((count, seqs, rows, LATENT), BF16)] * parts,
        scratch_shapes=[
            pltpu.VMEM((length, LATENT), F32),
            pltpu.VMEM((pairs, LATENT, 2 * HEAD), F32),
            pltpu.VMEM((pairs, LATENT, 2 * HEAD), F32),
        ],
        compiler_params=pltpu.CompilerParams(vmem_limit_bytes=VMEM_BYTES),
        cost_estimate=pl.CostEstimate(flops=flops, bytes_accessed=8 << 20, transcendentals=seqs * pairs * 2 * rows * length),
        name="attend_back",
    )(q, ql, mixed, lse, dval, uk, uv, keys, query_pos, key_pos)


def row_tiles(total, size):
    return [(at, min(size, total - at)) for at in range(0, total, size)]


def feed_kernel(*refs):
    rows_refs, dy_refs = refs[:4], refs[4:8]
    gate_ref, up_ref, down_ref, hidden_ref, dgate_ref, dup_ref, keep_ref, send_ref = refs[8:]
    rows = rows_refs[0].shape[0]
    for pair in (0, 1):
        left = jnp.concatenate([rows_refs[2 * pair][...], rows_refs[2 * pair + 1][...]])
        dy = jnp.concatenate([dy_refs[2 * pair][...], dy_refs[2 * pair + 1][...]])
        gate = product(left, gate_ref[...])
        up = product(left, up_ref[...])
        dhidden = times_transposed(dy, down_ref[...])
        sigmoid = 1.0 / (1.0 + jnp.exp(-gate))
        silu = gate * sigmoid
        span = slice(2 * pair * rows, 2 * (pair + 1) * rows)
        hidden_ref[span] = (silu * up).astype(BF16)
        dgate = (dhidden * up * (sigmoid * (1.0 + gate * (1.0 - sigmoid)))).astype(BF16)
        dup = (dhidden * silu).astype(BF16)
        dgate_ref[span] = dgate
        dup_ref[span] = dup
        shares = times_transposed(dgate, gate_ref[...]) + times_transposed(dup, up_ref[...])
        keep_ref[pair] = shares[:rows]
        send_ref[pair] = shares[rows:]


def feed_grads_kernel(*refs):
    rows_refs, dy_refs = refs[:4], refs[4:8]
    down_ref, hidden_ref, dgate_ref, dup_ref, ggate_ref, gup_ref, gdown_ref, keep_ref, send_ref = refs[8:]
    rows = rows_refs[0].shape[0]
    for at, size in row_tiles(rows_refs[0].shape[1], 256):
        left = jnp.concatenate([ref[:, at : at + size] for ref in rows_refs])
        ggate_ref[at : at + size] = contract_rows(left, dgate_ref[...]).astype(BF16)
        gup_ref[at : at + size] = contract_rows(left, dup_ref[...]).astype(BF16)
    dy = jnp.concatenate([ref[...] for ref in dy_refs])
    for at, size in row_tiles(hidden_ref.shape[1], 256):
        gdown_ref[at : at + size] = contract_rows(hidden_ref[:, at : at + size], dy).astype(BF16)
    for pair in (0, 1):
        shares = product(hidden_ref[2 * pair * rows : 2 * (pair + 1) * rows], down_ref[...])
        keep_ref[pair] = shares[:rows]
        send_ref[pair] = shares[rows:]


def feed(normed, dy, gate_full, up_full, down_full):
    rows, width = normed[0].shape
    units = gate_full.shape[1]
    low = jax.ShapeDtypeStruct((4 * rows, units), BF16)
    share = jax.ShapeDtypeStruct((2, rows, width), F32)
    flops = 2 * 4 * rows * width * units
    return pl.pallas_call(
        feed_kernel,
        out_shape=[low, low, low, share, share],
        in_specs=[pl.BlockSpec(memory_space=pltpu.VMEM)] * 11,
        out_specs=[pl.BlockSpec(memory_space=pltpu.VMEM)] * 5,
        compiler_params=pltpu.CompilerParams(vmem_limit_bytes=40 << 20),
        cost_estimate=pl.CostEstimate(flops=5 * flops, bytes_accessed=11 << 20, transcendentals=4 * rows * units),
        name="feed",
    )(*normed, *dy, gate_full, up_full, down_full)


def feed_grads(normed, dy, down_full, hidden, dgate, dup):
    rows, width = normed[0].shape
    units = hidden.shape[1]
    share = jax.ShapeDtypeStruct((2, rows, width), F32)
    flops = 2 * 4 * rows * width * units
    return pl.pallas_call(
        feed_grads_kernel,
        out_shape=[jax.ShapeDtypeStruct((width, units), BF16)] * 2
        + [jax.ShapeDtypeStruct((units, width), BF16), share, share],
        in_specs=[pl.BlockSpec(memory_space=pltpu.VMEM)] * 12,
        out_specs=[pl.BlockSpec(memory_space=pltpu.VMEM)] * 5,
        compiler_params=pltpu.CompilerParams(vmem_limit_bytes=40 << 20),
        cost_estimate=pl.CostEstimate(flops=4 * flops, bytes_accessed=14 << 20, transcendentals=0),
        name="feed_grads",
    )(*normed, *dy, down_full, hidden, dgate, dup)


class Plan:
    def __init__(self, mesh):
        self.dp, self.ctx = mesh.shape["dp"], mesh.shape["ctx"]
        self.count = self.dp * self.ctx
        self.core = self.ctx
        self.cross = 2 * self.ctx
        top = self.count // 2
        bits = [1 << n for n in range(self.count.bit_length() - 1)]
        ctx_bits = [b for b in bits if b < self.ctx]
        self.half_bits = [b for b in bits if b != self.core]
        self.split_bits = [self.core, self.cross]
        self.quarter_bits = [b for b in bits if b not in self.split_bits]
        self.ctx_bits = ctx_bits
        self.top = top

    def swap(self, value, mask):
        return lax.ppermute(value, AXES, [(n, n ^ mask) for n in range(self.count)])

    def swap_bits(self, number, first, second):
        if first == second:
            return number
        one, two = (number // first) % 2, (number // second) % 2
        return number + (two - one) * first + (one - two) * second

    def deal(self, value, pairs):
        table = []
        for n in range(self.count):
            m = n
            for first, second in pairs:
                m = self.swap_bits(m, first, second)
            table.append((n, m))
        if all(a == b for a, b in table):
            return value
        return lax.ppermute(value, AXES, table)


def masks_of(bits):
    out = [0]
    for bit in bits:
        out = out + [m ^ bit for m in out]
    return out


def gather(plan, value, far, bits, groups):
    done = [([m], value[None] if m == 0 else plan.swap(value, m)[None]) for m in masks_of(far)]
    for bit, count in zip(bits, groups):
        size = -(-len(done) // count)
        sent = []
        for at in range(0, len(done), size):
            some = done[at : at + size]
            masks = [m for ms, _ in some for m in ms]
            stack = some[0][1] if len(some) == 1 else jnp.concatenate([a for _, a in some])
            sent.append(([m ^ bit for m in masks], plan.swap(stack, bit)))
        done = done + sent
    return done


def reduce_order(far, second, first):
    base = masks_of(far)
    return [[m ^ one ^ two for m in base] for one in (0, first) for two in (0, second)]


def reduce_far(plan, part, far):
    total = part[0].astype(F32)
    for n, mask in enumerate(masks_of(far)):
        if n:
            total = total + plan.swap(part[n].astype(BF16), mask).astype(F32)
    return total


def reduce_near(plan, stacks, second, first):
    keep0, keep1, send0, send1 = stacks
    got1 = plan.swap(send1, first)
    got0 = plan.swap(send0, first)
    part1 = (keep1.astype(F32) + got1.astype(F32)).astype(BF16)
    got = plan.swap(part1, second)
    return (keep0.astype(F32) + got0.astype(F32) + got.astype(F32)).astype(BF16)


def tie(*values):
    return lax.optimization_barrier(values)


def per_device(plan, tokens, cotangent, domain_ids, domain_weights, stretch_offsets, gain_attn, gain_ffn,
               w_query, w_latent, w_upkey, w_upvalue, w_out, w_gate, w_up, w_down):
    _, rows, width = tokens.shape
    me = lax.axis_index("dp") * plan.ctx + lax.axis_index("ctx")
    here = lax.axis_index("ctx")
    core = (me // plan.core) % 2
    core_bit, cross_bit = plan.core, plan.cross
    count = plan.count
    shard = w_query.shape[0]
    up_shard = w_upkey.shape[0]
    down_shard = w_down.shape[0]
    half = w_query.shape[1] // 2
    latent_half = w_latent.shape[1] // 2
    pair_width = w_upkey.shape[1]
    quarter = w_gate.shape[1] // 4
    y_bit, *z_bits = plan.ctx_bits
    x_bit = plan.half_bits[-1]
    half_far = [b for b in plan.half_bits if b not in (x_bit, y_bit)]
    extra_bits = [b for b in plan.quarter_bits if b not in plan.ctx_bits]
    half_stages = (half_far, y_bit, x_bit)

    def halves(value, size):
        low, high = value[:, :size], value[:, size:]
        return jnp.where(core == 0, low, high), jnp.where(core == 0, high, low)

    query_own, query_other = halves(w_query, half)
    latent_own, latent_other = halves(w_latent, latent_half)
    info = jnp.concatenate([gain_attn, gain_ffn, stretch_offsets[0].astype(BF16)])
    info = jnp.pad(info[None], ((0, INFO - 1), (0, latent_half - info.shape[0])))
    band = shard + INFO
    folds = half // latent_half
    fold = lambda value: jnp.concatenate(jnp.split(value, folds, 1), 0)
    unfold = lambda value: jnp.concatenate(jnp.split(value, folds, 0), 1)
    got = plan.swap(jnp.concatenate([latent_other, info, fold(query_other)]), core_bit)
    first_message = jnp.concatenate([latent_own, info, got[:band]])
    dealt = plan.deal(
        jnp.concatenate([jnp.concatenate([w_upkey, w_upvalue], 1), w_out]), [(plan.top, core_bit)]
    )
    second_message = jnp.concatenate([jnp.concatenate([query_own, unfold(got[band:])], 1), dealt])
    split_masks = masks_of(plan.split_bits)
    split = (me // core_bit) % 2 + 2 * ((me // cross_bit) % 2)
    columns = jnp.concatenate([w_gate, w_up]).reshape(2 * shard, 4, quarter).transpose(1, 0, 2)

    def quarter_of(mask_index):
        return lax.dynamic_index_in_dim(columns, split ^ mask_index, 0, keepdims=False)

    down = plan.deal(w_down, [(plan.top, cross_bit), (plan.top // 2, core_bit)])
    low_width = min(quarter // 128 * 128, width)
    down_widths = [low_width, width - low_width]

    def narrow(value, column, columns):
        return jnp.pad(value[:, column : column + columns], ((0, 0), (0, quarter - columns)))

    third_message = jnp.concatenate(
        [quarter_of(0)]
        + [plan.swap(quarter_of(n), m) for n, m in enumerate(split_masks) if n]
        + [narrow(down, column, columns) for columns, column in bands_of(down_widths)]
    )
    columns_rows = 8 * shard
    third_rows = third_message.shape[0]

    tokens_two = jnp.concatenate([tokens[0], plan.swap(tokens[0], core_bit)])
    x_two = tokens_two.astype(F32)

    first_pieces = gather(plan, first_message, half_far, (y_bit, x_bit), (1, 1))
    second_pieces = gather(plan, second_message, half_far, (y_bit, x_bit), (4, 2))
    third_stack = jnp.concatenate([a for _, a in gather(plan, third_message, extra_bits, (), ())])
    extra_masks = masks_of(extra_bits)
    third_whole = lax.all_gather(third_stack, "ctx", axis=0, tiled=True)
    third_spots = [(c * len(extra_masks) + e, (me - here + c) ^ m) for c in range(plan.ctx) for e, m in enumerate(extra_masks)]

    def spots(pieces):
        return [(i, j, m) for i, (masks, _) in enumerate(pieces) for j, m in enumerate(masks)]

    def owner_half(number):
        return plan.swap_bits(number, plan.top, core_bit) % (count // 2)

    def owner_quarter(number):
        source = plan.swap_bits(number, plan.top // 2, core_bit)
        return plan.swap_bits(source, plan.top, cross_bit) % (count // 4)

    found = spots(first_pieces)
    (latent_full,) = place_blocks(
        [a for _, a in first_pieces],
        [[[(i, j, b * band, 0) for i, j, _ in found for b in (0, 1)]]],
        [[me ^ (m ^ b * core_bit) for _, _, m in found for b in (0, 1)]],
        [(shard, [latent_half])],
    )
    rows_info = jnp.concatenate(
        [a[:, shard :: band, : 2 * shard + 1] for _, a in first_pieces]
    )

    found = spots(second_pieces)
    owners = [owner_half(me ^ m) for _, _, m in found]
    query_full, upkey_full, upvalue_full, out_full = place_blocks(
        [a for _, a in second_pieces],
        [
            [[(i, j, 0, b * half) for i, j, _ in found for b in (0, 1)]],
            [[(i, j, shard, 0) for i, j, _ in found]],
            [[(i, j, shard, pair_width) for i, j, _ in found]],
            [[(i, j, shard + up_shard, 0) for i, j, _ in found]],
        ],
        [[me ^ (m ^ b * core_bit) for _, _, m in found for b in (0, 1)], owners, owners, owners],
        [(shard, [half]), (up_shard, [pair_width]), (up_shard, [pair_width]), (shard, [width])],
    )

    column_order = [number ^ s for _, number in third_spots for s in split_masks]
    down_order = [owner_quarter(number) for _, number in third_spots]
    third_blocks = [
        [[(0, j, n * 2 * shard, 0) for j, _ in third_spots for n in range(4)]],
        [[(0, j, n * 2 * shard + shard, 0) for j, _ in third_spots for n in range(4)]],
        [[(0, j, columns_rows + n * down_shard, 0) for j, _ in third_spots] for n in (0, 1)],
    ]
    third_orders = [column_order, column_order, down_order]
    third_shapes = [(shard, [quarter]), (shard, [quarter]), (down_shard, down_widths)]
    gate_full, up_full, down_full = place_blocks([third_whole], third_blocks, third_orders, third_shapes)

    masks_info = [m for _, _, m in spots(first_pieces)]
    number = jnp.stack([jnp.stack([me ^ m, me ^ m ^ core_bit]) for m in masks_info]).reshape(-1)
    chosen = (number[:, None] == jnp.arange(count)[None, :]).astype(BF16)
    gains = contract_rows(chosen, rows_info[..., : 2 * shard].reshape(count, 2 * shard))
    gain_one = gains[:, :shard].reshape(width)
    gain_two = gains[:, shard:].reshape(width)
    ctx_masks = [m ^ y for y in (0, y_bit) for m in masks_of(z_bits)]
    offsets = jnp.stack(
        [rows_info[masks_info.index(m), :, 2 * shard] for m in ctx_masks], 1
    ).astype(jnp.int32)
    within = jnp.arange(rows, dtype=jnp.int32)
    key_pos = (offsets[:, :, None] * rows + within).reshape(2, 1, -1)
    query_pos = (offsets[:, :1] * rows + within)[:, :, None]

    normed_one = (x_two * inverse_rms(x_two) * gain_one).astype(BF16)
    latent = product(normed_one, latent_full).astype(BF16)
    latent_message = latent.reshape(2, rows, latent_half)
    key_pieces = gather(plan, latent_message, z_bits, (y_bit,), (4,))
    key_of = {m: a[j] for masks, a in key_pieces for j, m in enumerate(masks)}
    keys = jnp.concatenate([key_of[m] for m in ctx_masks], 1)
    queries = product(normed_one, query_full).astype(BF16).reshape(2, rows, half)
    query_latent, mixed, lse, values = attend(queries, upkey_full, upvalue_full, keys, query_pos, key_pos)
    values = values.reshape(2 * rows, half)
    shares = product(values, out_full)
    x_own = x_two[:rows]
    middle = x_own + shares[:rows] + plan.swap(shares[rows:], core_bit)

    def spread(value):
        near = plan.swap(value, core_bit)
        across = plan.swap(value, cross_bit)
        return [value, near, across, plan.swap(across, core_bit)]

    def collect(keep, send):
        got = plan.swap(send, core_bit)
        across = plan.swap((keep[1] + got[1]).astype(BF16), cross_bit)
        return keep[0] + got[0] + across.astype(F32)

    match = domain_ids[:, None] == jnp.arange(DOMAINS, dtype=jnp.int32)[None, :]
    scale = jnp.sum(jnp.where(match, domain_weights[None, :], 0.0))
    dlayer = cotangent[0].astype(F32) * scale
    dy = spread(dlayer.astype(BF16))

    normed_two = spread((middle * inverse_rms(middle) * gain_two).astype(BF16))
    hidden, dgate, dup, keep, send = feed(normed_two, dy, gate_full, up_full, down_full)
    dnormed_two = collect(keep, send)
    grad_gate, grad_up, grad_down, keep, send = feed_grads(normed_two, dy, down_full, hidden, dgate, dup)
    output = (middle + collect(keep, send)).astype(BF16)[None]

    (third_grads,) = cut_blocks(
        [grad_gate, grad_up, grad_down], third_blocks, third_orders, third_shapes,
        [(len(third_spots), third_rows, quarter)],
        [(0, columns_rows + n * down_shard, down_shard, w, quarter - w) for n, w in enumerate(down_widths) if w < quarter],
    )
    third_sum = lax.psum_scatter(third_grads, "ctx", scatter_dimension=0, tiled=True)

    dmiddle_norm, grad_gain_two = norm_back(middle, gain_two, dnormed_two)
    dmiddle = dlayer + dmiddle_norm
    dm = dmiddle.astype(BF16)
    dm_two = jnp.concatenate([dm, plan.swap(dm, core_bit)])
    grad_out = contract_rows(values, dm_two).astype(BF16)
    dvalues = times_transposed(dm_two, out_full).astype(BF16).reshape(2, rows, half)
    dqueries, grad_upkey, grad_upvalue, keep, send = attend_back(
        queries, query_latent, mixed, lse, dvalues, upkey_full, upvalue_full, keys, query_pos, key_pos, 2
    )
    dlatent = reduce_far(plan, keep.astype(F32) + plan.swap(send, y_bit).astype(F32), z_bits)
    dlatent = dlatent.astype(BF16).reshape(2 * rows, latent_half)
    dqueries = dqueries.reshape(2 * rows, half)
    shares = times_transposed(dqueries, query_full) + times_transposed(dlatent, latent_full)
    dnormed_one = shares[:rows] + plan.swap(shares[rows:], core_bit)
    dx_norm, grad_gain_one = norm_back(x_own, gain_one, dnormed_one)
    grad_tokens = (dmiddle + dx_norm).astype(BF16)[None]

    half_order = reduce_order(*half_stages)
    places = [(i, j, m) for i, masks in enumerate(half_order) for j, m in enumerate(masks)]
    owners = [owner_half(me ^ m) for _, _, m in places]
    grad_query = contract_rows(normed_one, dqueries).astype(BF16)
    second_stacks = cut_blocks(
        [grad_query, grad_upkey, grad_upvalue, grad_out],
        [
            [[(i, j, 0, b * half) for i, j, _ in places for b in (0, 1)]],
            [[(i, j, shard, 0) for i, j, _ in places]],
            [[(i, j, shard, pair_width) for i, j, _ in places]],
            [[(i, j, shard + up_shard, 0) for i, j, _ in places]],
        ],
        [[me ^ (m ^ b * core_bit) for _, _, m in places for b in (0, 1)], owners, owners, owners],
        [(shard, [half]), (up_shard, [pair_width]), (up_shard, [pair_width]), (shard, [width])],
        [(len(masks),) + second_message.shape for masks in half_order],
    )
    second_part = reduce_near(plan, second_stacks, y_bit, x_bit)
    grad_latent = contract_rows(normed_one, dlatent).astype(BF16)
    gain_rows = jnp.concatenate([grad_gain_one.reshape(count, shard), grad_gain_two.reshape(count, shard)], 1)
    gain_rows = jnp.pad(gain_rows.astype(BF16)[:, None], ((0, 0), (0, INFO - 1), (0, latent_half - 2 * shard)))
    order = [me ^ (m ^ b * core_bit) for _, _, m in places for b in (0, 1)]
    first_stacks = cut_blocks(
        [grad_latent, gain_rows.reshape(count * INFO, latent_half)],
        [
            [[(i, j, b * band, 0) for i, j, _ in places for b in (0, 1)]],
            [[(i, j, b * band + shard, 0) for i, j, _ in places for b in (0, 1)]],
        ],
        [order, order],
        [(shard, [latent_half]), (INFO, [latent_half])],
        [(len(masks), 2 * band, latent_half) for masks in half_order],
    )
    first_part = reduce_near(plan, first_stacks, y_bit, x_bit)
    first_part, second_part, third_sum = tie(first_part, second_part, third_sum)
    third_sum = reduce_far(plan, third_sum, extra_bits) if extra_bits else third_sum[0] if third_sum.ndim == 3 else third_sum
    down_sum = third_sum[columns_rows:].reshape(2, down_shard, quarter)
    down_sum = jnp.concatenate([down_sum[n, :, :w] for n, w in enumerate(down_widths)], 1)
    grad_w_down = plan.deal(down_sum.astype(F32), [(plan.top // 2, core_bit), (plan.top, cross_bit)])
    column_sum = third_sum[:columns_rows].reshape(4, 2 * shard, quarter)
    got = jnp.stack(
        [column_sum[0]] + [plan.swap(column_sum[n].astype(BF16), m).astype(third_sum.dtype) for n, m in enumerate(split_masks) if n]
    )
    grad_columns = jnp.concatenate(
        [lax.dynamic_index_in_dim(got, split ^ n, 0, keepdims=False) for n in range(4)], 1
    ).astype(F32)
    grad_w_gate, grad_w_up = grad_columns[:shard], grad_columns[shard:]
    first_sum = reduce_far(plan, first_part, half_far)
    second_sum = reduce_far(plan, second_part, half_far)
    own, got = second_sum[:shard, :half], plan.swap(second_sum[:shard, half:].astype(BF16), core_bit).astype(F32)
    grad_w_query = jnp.concatenate([jnp.where(core == 0, own, got), jnp.where(core == 0, got, own)], 1)
    dealt = plan.deal(second_sum[shard:].astype(BF16), [(plan.top, core_bit)]).astype(F32)
    grad_w_out = dealt[up_shard:]
    own, got = first_sum[:band], plan.swap(first_sum[band:].astype(BF16), core_bit).astype(F32)
    grad_w_latent = jnp.concatenate([jnp.where(core == 0, own, got), jnp.where(core == 0, got, own)], 1)[:shard]
    gain_sums = own[shard] + got[shard]

    return (
        output, grad_tokens, gain_sums[:shard], gain_sums[shard : 2 * shard],
        grad_w_query, grad_w_latent, dealt[:up_shard, :pair_width], dealt[:up_shard, pair_width:],
        grad_w_out, grad_w_gate, grad_w_up, grad_w_down,
    )


def solution(mesh):
    rows = P(("dp", "ctx"), None)
    vector = P(("dp", "ctx"))
    stretch = P("dp", "ctx", None)
    in_specs = (stretch, stretch, P("dp"), P(), P("dp", "ctx"), vector, vector) + (rows,) * 8
    out_specs = (stretch, stretch, vector, vector) + (rows,) * 8
    return jax.shard_map(
        functools.partial(per_device, Plan(mesh)), mesh=mesh, in_specs=in_specs, out_specs=out_specs,
        check_vma=False,
    )
```

```python
import functools
import itertools
import math

import jax
import jax.numpy as jnp
from jax import lax
from jax.experimental import pallas as pl
from jax.experimental.pallas import tpu as pltpu
from jax.sharding import PartitionSpec as P

PAIRS_A_STEP = 2
HEAD = 64
LATENT = 256
DOMAINS = 8
EPS = 1e-06
SCALE = 0.125
MASKED = -1e30
AXES = ("dp", "ctx")
BF16 = jnp.bfloat16
F32 = jnp.float32
INFO = 8
VMEM_BYTES = 56 * 1024 * 1024


def product(left, right):
    return jnp.dot(left, right, preferred_element_type=F32)


def contract_rows(left, right):
    return lax.dot_general(left, right, (((0,), (0,)), ((), ())), preferred_element_type=F32)


def times_transposed(left, right):
    return lax.dot_general(left, right, (((1,), (1,)), ((), ())), preferred_element_type=F32)


def inverse_rms(rows):
    return lax.rsqrt(jnp.mean(rows * rows, -1, keepdims=True) + EPS)


def norm_back(rows, gain, grad):
    r = inverse_rms(rows)
    grad_gain = jnp.sum(grad * rows * r, 0)
    scaled = grad * gain
    mean = jnp.mean(scaled * rows, -1, keepdims=True)
    return r * scaled - rows * (r * r * r * mean), grad_gain


def groups_of(spots):
    groups = {}
    for n, (i, j, r, k) in enumerate(spots):
        groups.setdefault((i, r, k), []).append((j, n))
    return [(key, [n for _, n in sorted(found)]) for key, found in groups.items()]


def permute_blocks(chosen, stack):
    out = product(chosen.astype(BF16), stack.reshape(stack.shape[0], -1)).astype(BF16)
    return out.reshape(-1, *stack.shape[1:])


def bands_of(widths):
    return list(zip(widths, itertools.accumulate([0, *widths[:-1]])))


def kernel_bytes(shapes):
    return 4 * sum(math.prod(shape) for shape in shapes) + (4 << 20)


def place_blocks(pieces, blocks, orders, shapes):
    if any(rows % 8 for rows, _ in shapes):
        made = []
        for (rows, widths), bands, order in zip(shapes, blocks, orders):
            parts = []
            for (width, _), spots in zip(bands_of(widths), bands):
                groups = groups_of(spots)
                stack = jnp.concatenate([pieces[i][:, r : r + rows, k : k + width] for (i, r, k), _ in groups])
                own = jnp.stack([order[n] for _, ns in groups for n in ns])
                numbers = jnp.arange(len(spots), dtype=own.dtype)
                parts.append(permute_blocks(own[None, :] == numbers[:, None], stack))
            made.append(jnp.concatenate(parts, 2).reshape(-1, sum(widths)))
        return made

    def kernel(order_ref, *refs):
        sources, targets = refs[: len(pieces)], refs[len(pieces) :]
        first = 0
        for target, (rows, widths), bands in zip(targets, shapes, blocks):
            for (width, column), spots in zip(bands_of(widths), bands):
                for n, (i, j, r, k) in enumerate(spots):
                    target[order_ref[first + n], :, column : column + width] = sources[i][
                        j, r : r + rows, k : k + width
                    ]
            first += len(bands[0])

    out_shapes = [(len(bands[0]), rows, sum(widths)) for (rows, widths), bands in zip(shapes, blocks)]
    made = pl.pallas_call(
        kernel,
        out_shape=[jax.ShapeDtypeStruct(shape, BF16) for shape in out_shapes],
        in_specs=[pl.BlockSpec(memory_space=pltpu.SMEM)]
        + [pl.BlockSpec(memory_space=pltpu.VMEM)] * len(pieces),
        out_specs=[pl.BlockSpec(memory_space=pltpu.VMEM)] * len(shapes),
        compiler_params=pltpu.CompilerParams(
            vmem_limit_bytes=kernel_bytes(out_shapes + [p.shape for p in pieces])
        ),
        name="place_blocks",
    )(jnp.stack([n for order in orders for n in order]), *pieces)
    return [whole.reshape(-1, whole.shape[-1]) for whole in made]


def cut_blocks(matrices, blocks, orders, shapes, piece_shapes, spare=()):
    if any(rows % 8 for rows, _ in shapes):
        bands_at = [{} for _ in piece_shapes]
        for (rows, widths), bands, order, matrix in zip(shapes, blocks, orders, matrices):
            grid = matrix.reshape(len(bands[0]), rows, -1)
            for (width, column), spots in zip(bands_of(widths), bands):
                for (i, r, k), ns in groups_of(spots):
                    own = jnp.stack([order[n] for n in ns])
                    chosen = own[:, None] == jnp.arange(len(spots), dtype=own.dtype)[None, :]
                    bands_at[i].setdefault(r, {})[k] = permute_blocks(chosen, grid[:, :, column : column + width])
        for i, r, rows, k, columns in spare:
            bands_at[i].setdefault(r, {})[k] = jnp.zeros((piece_shapes[i][0], rows, columns), BF16)
        return [
            jnp.concatenate(
                [jnp.concatenate([row[k] for k in sorted(row)], 2) for _, row in sorted(band.items())], 1
            )
            for band in bands_at
        ]

    def kernel(order_ref, *refs):
        sources, targets = refs[: len(matrices)], refs[len(matrices) :]
        for i, r, rows, k, columns in spare:
            targets[i][:, r : r + rows, k : k + columns] = jnp.zeros((piece_shapes[i][0], rows, columns), BF16)
        first = 0
        for source, (rows, widths), bands in zip(sources, shapes, blocks):
            for (width, column), spots in zip(bands_of(widths), bands):
                for n, (i, j, r, k) in enumerate(spots):
                    targets[i][j, r : r + rows, k : k + width] = source[
                        order_ref[first + n], :, column : column + width
                    ]
            first += len(bands[0])

    grids = [matrix.reshape(-1, rows, matrix.shape[-1]) for matrix, (rows, _) in zip(matrices, shapes)]
    return pl.pallas_call(
        kernel,
        out_shape=[jax.ShapeDtypeStruct(shape, BF16) for shape in piece_shapes],
        in_specs=[pl.BlockSpec(memory_space=pltpu.SMEM)]
        + [pl.BlockSpec(memory_space=pltpu.VMEM)] * len(matrices),
        out_specs=[pl.BlockSpec(memory_space=pltpu.VMEM)] * len(piece_shapes),
        compiler_params=pltpu.CompilerParams(
            vmem_limit_bytes=kernel_bytes(list(piece_shapes) + [g.shape for g in grids])
        ),
        name="cut_blocks",
    )(jnp.stack([n for order in orders for n in order]), *grids)


def pair_scores(query_latent, keys, visible):
    scores = times_transposed(query_latent * jnp.asarray(SCALE, BF16), keys)
    return jnp.where(visible, scores, MASKED)


def visible_keys(query_pos, key_pos):
    return jnp.concatenate([query_pos, query_pos], 0) >= key_pos


def pair_lanes(n):
    return slice(2 * n * HEAD, 2 * (n + 1) * HEAD)


def attend_kernel(q_ref, uk_ref, uv_ref, keys_ref, qpos_ref, kpos_ref, ql_ref, mixed_ref, lse_ref, values_ref):
    keys = keys_ref[0]
    visible = visible_keys(qpos_ref[0], kpos_ref[0])
    for n in range(ql_ref.shape[1]):
        lanes = pair_lanes(n)
        q, uk, uv = q_ref[0][:, lanes], uk_ref[:, lanes], uv_ref[:, lanes]
        rows = q.shape[0]
        ql = jnp.concatenate(
            [times_transposed(q[:, k : k + HEAD], uk[:, k : k + HEAD]) for k in (0, HEAD)], 0
        ).astype(BF16)
        scores = pair_scores(ql, keys, visible)
        top = jnp.max(scores, -1, keepdims=True)
        terms = jnp.exp(scores - top)
        total = jnp.sum(terms, -1, keepdims=True)
        probs = (terms * (1.0 / total)).astype(BF16)
        mixed = product(probs, keys).astype(BF16)
        ql_ref[0, n] = ql
        mixed_ref[0, n] = mixed
        lse_ref[0, n] = top + jnp.log(total)
        values_ref[0, :, lanes] = jnp.concatenate(
            [product(mixed[:rows], uv[:, :HEAD]), product(mixed[rows:], uv[:, HEAD:])], 1
        ).astype(BF16)


def attend_back_kernel(
    q_ref, ql_ref, mixed_ref, lse_ref, dval_ref, uk_ref, uv_ref, keys_ref, qpos_ref, kpos_ref,
    dq_ref, guk_ref, guv_ref, *rest,
):
    dkeys_refs, (keys_acc, uk_acc, uv_acc) = rest[:-3], rest[-3:]
    seq, step = pl.program_id(0), pl.program_id(1)
    keys = keys_ref[0]
    visible = visible_keys(qpos_ref[0], kpos_ref[0])
    halves = (0, HEAD)
    inside = ql_ref.shape[1]
    dkeys = None
    for n in range(inside):
        lanes = pair_lanes(n)
        q, dval, uk, uv = q_ref[0][:, lanes], dval_ref[0][:, lanes], uk_ref[:, lanes], uv_ref[:, lanes]
        ql, mixed = ql_ref[0, n], mixed_ref[0, n]
        rows = q.shape[0]
        scores = pair_scores(ql, keys, visible)
        probs = jnp.exp(scores - lse_ref[0, n])
        dmixed = jnp.concatenate(
            [times_transposed(dval[:, k : k + HEAD], uv[:, k : k + HEAD]) for k in halves], 0
        ).astype(BF16)
        dprobs = times_transposed(dmixed, keys)
        dscores = probs * (dprobs - jnp.sum(probs * dprobs, -1, keepdims=True))
        dscores = dscores.astype(BF16) * jnp.asarray(SCALE, BF16)
        dql = product(dscores, keys).astype(BF16)
        part = contract_rows(dscores, ql) + contract_rows(probs.astype(BF16), dmixed)
        dkeys = part if dkeys is None else dkeys + part
        guk = jnp.concatenate(
            [contract_rows(dql[i * rows : (i + 1) * rows], q[:, k : k + HEAD]) for i, k in enumerate(halves)], 1
        )
        guv = jnp.concatenate(
            [contract_rows(mixed[i * rows : (i + 1) * rows], dval[:, k : k + HEAD]) for i, k in enumerate(halves)], 1
        )
        pair = step * inside + n
        uk_acc[pair] = jnp.where(seq == 0, guk, uk_acc[pair] + guk)
        uv_acc[pair] = jnp.where(seq == 0, guv, uv_acc[pair] + guv)
        dq_ref[0, :, lanes] = jnp.concatenate(
            [product(dql[i * rows : (i + 1) * rows], uk[:, k : k + HEAD]) for i, k in enumerate(halves)], 1
        ).astype(BF16)

    @pl.when(step == 0)
    def _():
        keys_acc[...] = dkeys

    @pl.when(step > 0)
    def _():
        keys_acc[...] += dkeys

    last = pl.num_programs(1) - 1

    @pl.when(step == last)
    def _():
        count = dkeys_refs[0].shape[0]
        for n, ref in enumerate(dkeys_refs):
            part = keys_acc[n * count * rows : (n + 1) * count * rows, :]
            ref[:, 0] = part.reshape(count, rows, LATENT).astype(BF16)

    @pl.when((step == last) & (seq == pl.num_programs(0) - 1))
    def _():
        for n in range(uk_acc.shape[0]):
            guk_ref[:, pair_lanes(n)] = uk_acc[n].astype(BF16)
            guv_ref[:, pair_lanes(n)] = uv_acc[n].astype(BF16)


def attention_specs(length, rows):
    pair = pl.BlockSpec((1, rows, 2 * PAIRS_A_STEP * HEAD), lambda s, p: (s, 0, p))
    up = pl.BlockSpec((LATENT, 2 * PAIRS_A_STEP * HEAD), lambda s, p: (0, p))
    keys = pl.BlockSpec((1, length, LATENT), lambda s, p: (s, 0, 0))
    query_pos = pl.BlockSpec((1, rows, 1), lambda s, p: (s, 0, 0))
    key_pos = pl.BlockSpec((1, 1, length), lambda s, p: (s, 0, 0))
    wide = pl.BlockSpec((1, PAIRS_A_STEP, 2 * rows, LATENT), lambda s, p: (s, p, 0, 0))
    thin = pl.BlockSpec((1, PAIRS_A_STEP, 2 * rows, 1), lambda s, p: (s, p, 0, 0))
    return pair, up, keys, query_pos, key_pos, wide, thin


def attend(q, uk, uv, keys, query_pos, key_pos):
    seqs, length, _ = keys.shape
    rows, pairs = q.shape[1], q.shape[2] // (2 * HEAD)
    pair, up, key, qpos, kpos, wide, thin = attention_specs(length, rows)
    flops = seqs * pairs * 2 * rows * length * LATENT * 4
    return pl.pallas_call(
        attend_kernel,
        grid=(seqs, pairs // PAIRS_A_STEP),
        in_specs=[pair, up, up, key, qpos, kpos],
        out_specs=[wide, wide, thin, pair],
        out_shape=[
            jax.ShapeDtypeStruct((seqs, pairs, 2 * rows, LATENT), BF16),
            jax.ShapeDtypeStruct((seqs, pairs, 2 * rows, LATENT), BF16),
            jax.ShapeDtypeStruct((seqs, pairs, 2 * rows, 1), F32),
            jax.ShapeDtypeStruct(q.shape, BF16),
        ],
        compiler_params=pltpu.CompilerParams(vmem_limit_bytes=VMEM_BYTES),
        cost_estimate=pl.CostEstimate(flops=flops, bytes_accessed=6 << 20, transcendentals=seqs * pairs * 2 * rows * length),
        name="attend",
    )(q, uk, uv, keys, query_pos, key_pos)


def attend_back(q, ql, mixed, lse, dval, uk, uv, keys, query_pos, key_pos, parts):
    seqs, length, _ = keys.shape
    rows, pairs = q.shape[1], q.shape[2] // (2 * HEAD)
    pair, up, key, qpos, kpos, wide, thin = attention_specs(length, rows)
    whole = pl.BlockSpec(uk.shape, lambda s, p: (0, 0))
    count = length // rows // parts
    flops = seqs * pairs * 2 * rows * length * LATENT * 10
    return pl.pallas_call(
        attend_back_kernel,
        grid=(seqs, pairs // PAIRS_A_STEP),
        in_specs=[pair, wide, wide, thin, pair, up, up, key, qpos, kpos],
        out_specs=[pair, whole, whole]
        + [pl.BlockSpec((count, 1, rows, LATENT), lambda s, p: (0, s, 0, 0))] * parts,
        out_shape=[jax.ShapeDtypeStruct(q.shape, BF16)]
        + [jax.ShapeDtypeStruct(uk.shape, BF16)] * 2
        + [jax.ShapeDtypeStruct((count, seqs, rows, LATENT), BF16)] * parts,
        scratch_shapes=[
            pltpu.VMEM((length, LATENT), F32),
            pltpu.VMEM((pairs, LATENT, 2 * HEAD), F32),
            pltpu.VMEM((pairs, LATENT, 2 * HEAD), F32),
        ],
        compiler_params=pltpu.CompilerParams(vmem_limit_bytes=VMEM_BYTES),
        cost_estimate=pl.CostEstimate(flops=flops, bytes_accessed=8 << 20, transcendentals=seqs * pairs * 2 * rows * length),
        name="attend_back",
    )(q, ql, mixed, lse, dval, uk, uv, keys, query_pos, key_pos)


def row_tiles(total, size):
    return [(at, min(size, total - at)) for at in range(0, total, size)]


def fetch_rows(sources, buffer, sem):
    rows = sources[0].shape[0]
    copies = [
        pltpu.make_async_copy(source, buffer.at[pl.ds(n * rows, rows), :], sem.at[n])
        for n, source in enumerate(sources)
    ]
    for copy in copies:
        copy.start()
    return copies


def feed_kernel(*refs):
    sources = refs[:8]
    gate_ref, up_ref, down_ref, hidden_ref, dgate_ref, dup_ref, keep_ref, send_ref, buffer, sem = refs[8:]
    rows = sources[0].shape[0]
    copies = fetch_rows(sources, buffer, sem)
    for pair in (0, 1):
        for n in (2 * pair, 2 * pair + 1, 2 * pair + 4, 2 * pair + 5):
            copies[n].wait()
        left = buffer[2 * pair * rows : 2 * (pair + 1) * rows]
        dy = buffer[(2 * pair + 4) * rows : (2 * pair + 6) * rows]
        gate = product(left, gate_ref[...])
        up = product(left, up_ref[...])
        dhidden = times_transposed(dy, down_ref[...])
        sigmoid = 1.0 / (1.0 + jnp.exp(-gate))
        silu = gate * sigmoid
        span = slice(2 * pair * rows, 2 * (pair + 1) * rows)
        hidden_ref[span] = (silu * up).astype(BF16)
        dgate = (dhidden * up * (sigmoid * (1.0 + gate * (1.0 - sigmoid)))).astype(BF16)
        dup = (dhidden * silu).astype(BF16)
        dgate_ref[span] = dgate
        dup_ref[span] = dup
        shares = times_transposed(dgate, gate_ref[...]) + times_transposed(dup, up_ref[...])
        keep_ref[pair] = shares[:rows]
        send_ref[pair] = shares[rows:]


def feed_grads_kernel(*refs):
    sources = refs[:8]
    down_ref, hidden_ref, dgate_ref, dup_ref, ggate_ref, gup_ref, gdown_ref, keep_ref, send_ref, buffer, sem = refs[8:]
    rows = sources[0].shape[0]
    for copy in fetch_rows(sources, buffer, sem):
        copy.wait()
    for at, size in row_tiles(buffer.shape[1], 256):
        left = buffer[: 4 * rows, at : at + size]
        ggate_ref[at : at + size] = contract_rows(left, dgate_ref[...]).astype(BF16)
        gup_ref[at : at + size] = contract_rows(left, dup_ref[...]).astype(BF16)
    dy = buffer[4 * rows :]
    for at, size in row_tiles(hidden_ref.shape[1], 256):
        gdown_ref[at : at + size] = contract_rows(hidden_ref[:, at : at + size], dy).astype(BF16)
    for pair in (0, 1):
        shares = product(hidden_ref[2 * pair * rows : 2 * (pair + 1) * rows], down_ref[...])
        keep_ref[pair] = shares[:rows]
        send_ref[pair] = shares[rows:]


def feed(normed, dy, gate_full, up_full, down_full):
    rows, width = normed[0].shape
    units = gate_full.shape[1]
    low = jax.ShapeDtypeStruct((4 * rows, units), BF16)
    share = jax.ShapeDtypeStruct((2, rows, width), F32)
    flops = 2 * 4 * rows * width * units
    return pl.pallas_call(
        feed_kernel,
        out_shape=[low, low, low, share, share],
        in_specs=[pl.BlockSpec(memory_space=pl.ANY)] * 8 + [pl.BlockSpec(memory_space=pltpu.VMEM)] * 3,
        out_specs=[pl.BlockSpec(memory_space=pltpu.VMEM)] * 5,
        scratch_shapes=[pltpu.VMEM((8 * rows, width), BF16), pltpu.SemaphoreType.DMA((8,))],
        compiler_params=pltpu.CompilerParams(vmem_limit_bytes=40 << 20),
        cost_estimate=pl.CostEstimate(flops=5 * flops, bytes_accessed=11 << 20, transcendentals=4 * rows * units),
        name="feed",
    )(*normed, *dy, gate_full, up_full, down_full)


def feed_grads(normed, dy, down_full, hidden, dgate, dup):
    rows, width = normed[0].shape
    units = hidden.shape[1]
    share = jax.ShapeDtypeStruct((2, rows, width), F32)
    flops = 2 * 4 * rows * width * units
    return pl.pallas_call(
        feed_grads_kernel,
        out_shape=[jax.ShapeDtypeStruct((width, units), BF16)] * 2
        + [jax.ShapeDtypeStruct((units, width), BF16), share, share],
        in_specs=[pl.BlockSpec(memory_space=pl.ANY)] * 8 + [pl.BlockSpec(memory_space=pltpu.VMEM)] * 4,
        out_specs=[pl.BlockSpec(memory_space=pltpu.VMEM)] * 5,
        scratch_shapes=[pltpu.VMEM((8 * rows, width), BF16), pltpu.SemaphoreType.DMA((8,))],
        compiler_params=pltpu.CompilerParams(vmem_limit_bytes=40 << 20),
        cost_estimate=pl.CostEstimate(flops=4 * flops, bytes_accessed=14 << 20, transcendentals=0),
        name="feed_grads",
    )(*normed, *dy, down_full, hidden, dgate, dup)


class Plan:
    def __init__(self, mesh):
        self.dp, self.ctx = mesh.shape["dp"], mesh.shape["ctx"]
        self.count = self.dp * self.ctx
        self.core = self.ctx
        self.cross = 2 * self.ctx
        top = self.count // 2
        bits = [1 << n for n in range(self.count.bit_length() - 1)]
        ctx_bits = [b for b in bits if b < self.ctx]
        self.half_bits = [b for b in bits if b != self.core]
        self.split_bits = [self.core, self.cross]
        self.quarter_bits = [b for b in bits if b not in self.split_bits]
        self.ctx_bits = ctx_bits
        self.top = top

    def swap(self, value, mask):
        return lax.ppermute(value, AXES, [(n, n ^ mask) for n in range(self.count)])

    def swap_bits(self, number, first, second):
        if first == second:
            return number
        one, two = (number // first) % 2, (number // second) % 2
        return number + (two - one) * first + (one - two) * second

    def deal(self, value, pairs):
        table = []
        for n in range(self.count):
            m = n
            for first, second in pairs:
                m = self.swap_bits(m, first, second)
            table.append((n, m))
        if all(a == b for a, b in table):
            return value
        return lax.ppermute(value, AXES, table)


def masks_of(bits):
    out = [0]
    for bit in bits:
        out = out + [m ^ bit for m in out]
    return out


def gather(plan, value, far, bits, groups):
    done = [([m], value[None] if m == 0 else plan.swap(value, m)[None]) for m in masks_of(far)]
    for bit, count in zip(bits, groups):
        size = -(-len(done) // count)
        sent = []
        for at in range(0, len(done), size):
            some = done[at : at + size]
            masks = [m for ms, _ in some for m in ms]
            stack = some[0][1] if len(some) == 1 else jnp.concatenate([a for _, a in some])
            sent.append(([m ^ bit for m in masks], plan.swap(stack, bit)))
        done = done + sent
    return done


def reduce_order(far, second, first):
    base = masks_of(far)
    return [[m ^ one ^ two for m in base] for one in (0, first) for two in (0, second)]


def reduce_far(plan, part, far):
    total = part[0].astype(F32)
    for n, mask in enumerate(masks_of(far)):
        if n:
            total = total + plan.swap(part[n].astype(BF16), mask).astype(F32)
    return total


def reduce_near(plan, stacks, second, first):
    keep0, keep1, send0, send1 = stacks
    got1 = plan.swap(send1, first)
    got0 = plan.swap(send0, first)
    part1 = (keep1.astype(F32) + got1.astype(F32)).astype(BF16)
    got = plan.swap(part1, second)
    return (keep0.astype(F32) + got0.astype(F32) + got.astype(F32)).astype(BF16)


def tie(*values):
    return lax.optimization_barrier(values)


def per_device(plan, tokens, cotangent, domain_ids, domain_weights, stretch_offsets, gain_attn, gain_ffn,
               w_query, w_latent, w_upkey, w_upvalue, w_out, w_gate, w_up, w_down):
    _, rows, width = tokens.shape
    me = lax.axis_index("dp") * plan.ctx + lax.axis_index("ctx")
    here = lax.axis_index("ctx")
    core = (me // plan.core) % 2
    core_bit, cross_bit = plan.core, plan.cross
    count = plan.count
    shard = w_query.shape[0]
    up_shard = w_upkey.shape[0]
    down_shard = w_down.shape[0]
    half = w_query.shape[1] // 2
    latent_half = w_latent.shape[1] // 2
    pair_width = w_upkey.shape[1]
    quarter = w_gate.shape[1] // 4
    y_bit, *z_bits = plan.ctx_bits
    x_bit = plan.half_bits[-1]
    half_far = [b for b in plan.half_bits if b not in (x_bit, y_bit)]
    extra_bits = [b for b in plan.quarter_bits if b not in plan.ctx_bits]
    half_stages = (half_far, y_bit, x_bit)

    def halves(value, size):
        low, high = value[:, :size], value[:, size:]
        return jnp.where(core == 0, low, high), jnp.where(core == 0, high, low)

    query_own, query_other = halves(w_query, half)
    latent_own, latent_other = halves(w_latent, latent_half)
    info = jnp.concatenate([gain_attn, gain_ffn, stretch_offsets[0].astype(BF16)])
    info = jnp.pad(info[None], ((0, INFO - 1), (0, latent_half - info.shape[0])))
    band = shard + INFO
    folds = half // latent_half
    fold = lambda value: jnp.concatenate(jnp.split(value, folds, 1), 0)
    unfold = lambda value: jnp.concatenate(jnp.split(value, folds, 0), 1)
    got = plan.swap(jnp.concatenate([latent_other, info, fold(query_other)]), core_bit)
    first_message = jnp.concatenate([latent_own, info, got[:band]])
    dealt = plan.deal(
        jnp.concatenate([jnp.concatenate([w_upkey, w_upvalue], 1), w_out]), [(plan.top, core_bit)]
    )
    second_message = jnp.concatenate([jnp.concatenate([query_own, unfold(got[band:])], 1), dealt])
    split_masks = masks_of(plan.split_bits)
    split = (me // core_bit) % 2 + 2 * ((me // cross_bit) % 2)
    columns = jnp.concatenate([w_gate, w_up]).reshape(2 * shard, 4, quarter).transpose(1, 0, 2)

    def quarter_of(mask_index):
        return lax.dynamic_index_in_dim(columns, split ^ mask_index, 0, keepdims=False)

    down = plan.deal(w_down, [(plan.top, cross_bit), (plan.top // 2, core_bit)])
    low_width = min(quarter // 128 * 128, width)
    down_widths = [low_width, width - low_width]

    def narrow(value, column, columns):
        return jnp.pad(value[:, column : column + columns], ((0, 0), (0, quarter - columns)))

    third_message = jnp.concatenate(
        [quarter_of(0)]
        + [plan.swap(quarter_of(n), m) for n, m in enumerate(split_masks) if n]
        + [narrow(down, column, columns) for columns, column in bands_of(down_widths)]
    )
    columns_rows = 8 * shard
    third_rows = third_message.shape[0]

    tokens_two = jnp.concatenate([tokens[0], plan.swap(tokens[0], core_bit)])
    x_two = tokens_two.astype(F32)

    first_pieces = gather(plan, first_message, half_far, (y_bit, x_bit), (1, 1))
    second_pieces = gather(plan, second_message, half_far, (y_bit, x_bit), (4, 1))
    third_stack = jnp.concatenate([a for _, a in gather(plan, third_message, extra_bits, (), ())])
    extra_masks = masks_of(extra_bits)
    third_whole = lax.all_gather(third_stack, "ctx", axis=0, tiled=True)
    third_spots = [(c * len(extra_masks) + e, (me - here + c) ^ m) for c in range(plan.ctx) for e, m in enumerate(extra_masks)]

    def spots(pieces):
        return [(i, j, m) for i, (masks, _) in enumerate(pieces) for j, m in enumerate(masks)]

    def owner_half(number):
        return plan.swap_bits(number, plan.top, core_bit) % (count // 2)

    def owner_quarter(number):
        source = plan.swap_bits(number, plan.top // 2, core_bit)
        return plan.swap_bits(source, plan.top, cross_bit) % (count // 4)

    found = spots(first_pieces)
    (latent_full,) = place_blocks(
        [a for _, a in first_pieces],
        [[[(i, j, b * band, 0) for i, j, _ in found for b in (0, 1)]]],
        [[me ^ (m ^ b * core_bit) for _, _, m in found for b in (0, 1)]],
        [(shard, [latent_half])],
    )
    rows_info = jnp.concatenate(
        [a[:, shard :: band, : 2 * shard + 1] for _, a in first_pieces]
    )

    found = spots(second_pieces)
    owners = [owner_half(me ^ m) for _, _, m in found]
    query_full, upkey_full, upvalue_full, out_full = place_blocks(
        [a for _, a in second_pieces],
        [
            [[(i, j, 0, b * half) for i, j, _ in found for b in (0, 1)]],
            [[(i, j, shard, 0) for i, j, _ in found]],
            [[(i, j, shard, pair_width) for i, j, _ in found]],
            [[(i, j, shard + up_shard, 0) for i, j, _ in found]],
        ],
        [[me ^ (m ^ b * core_bit) for _, _, m in found for b in (0, 1)], owners, owners, owners],
        [(shard, [half]), (up_shard, [pair_width]), (up_shard, [pair_width]), (shard, [width])],
    )

    column_order = [number ^ s for _, number in third_spots for s in split_masks]
    down_order = [owner_quarter(number) for _, number in third_spots]
    third_blocks = [
        [[(0, j, n * 2 * shard, 0) for j, _ in third_spots for n in range(4)]],
        [[(0, j, n * 2 * shard + shard, 0) for j, _ in third_spots for n in range(4)]],
        [[(0, j, columns_rows + n * down_shard, 0) for j, _ in third_spots] for n in (0, 1)],
    ]
    third_orders = [column_order, column_order, down_order]
    third_shapes = [(shard, [quarter]), (shard, [quarter]), (down_shard, down_widths)]
    gate_full, up_full, down_full = place_blocks([third_whole], third_blocks, third_orders, third_shapes)

    masks_info = [m for _, _, m in spots(first_pieces)]
    number = jnp.stack([jnp.stack([me ^ m, me ^ m ^ core_bit]) for m in masks_info]).reshape(-1)
    chosen = (number[:, None] == jnp.arange(count)[None, :]).astype(BF16)
    gains = contract_rows(chosen, rows_info[..., : 2 * shard].reshape(count, 2 * shard))
    gain_one = gains[:, :shard].reshape(width)
    gain_two = gains[:, shard:].reshape(width)
    ctx_masks = [m ^ y for y in (0, y_bit) for m in masks_of(z_bits)]
    offsets = jnp.stack(
        [rows_info[masks_info.index(m), :, 2 * shard] for m in ctx_masks], 1
    ).astype(jnp.int32)
    within = jnp.arange(rows, dtype=jnp.int32)
    key_pos = (offsets[:, :, None] * rows + within).reshape(2, 1, -1)
    query_pos = (offsets[:, :1] * rows + within)[:, :, None]

    normed_one = (x_two * inverse_rms(x_two) * gain_one).astype(BF16)
    latent = product(normed_one, latent_full).astype(BF16)
    latent_message = latent.reshape(2, rows, latent_half)
    key_pieces = gather(plan, latent_message, z_bits, (y_bit,), (4,))
    key_of = {m: a[j] for masks, a in key_pieces for j, m in enumerate(masks)}
    keys = jnp.concatenate([key_of[m] for m in ctx_masks], 1)
    queries = product(normed_one, query_full).astype(BF16).reshape(2, rows, half)
    query_latent, mixed, lse, values = attend(queries, upkey_full, upvalue_full, keys, query_pos, key_pos)
    values = values.reshape(2 * rows, half)
    shares = product(values, out_full)
    x_own = x_two[:rows]
    middle = x_own + shares[:rows] + plan.swap(shares[rows:], core_bit)

    def spread(value):
        near = plan.swap(value, core_bit)
        across = plan.swap(value, cross_bit)
        return [value, near, across, plan.swap(across, core_bit)]

    def collect(keep, send):
        got = plan.swap(send, core_bit)
        across = plan.swap((keep[1] + got[1]).astype(BF16), cross_bit)
        return keep[0] + got[0] + across.astype(F32)

    match = domain_ids[:, None] == jnp.arange(DOMAINS, dtype=jnp.int32)[None, :]
    scale = jnp.sum(jnp.where(match, domain_weights[None, :], 0.0))
    dlayer = cotangent[0].astype(F32) * scale
    dy = spread(dlayer.astype(BF16))

    normed_two = spread((middle * inverse_rms(middle) * gain_two).astype(BF16))
    hidden, dgate, dup, keep, send = feed(normed_two, dy, gate_full, up_full, down_full)
    dnormed_two = collect(keep, send)
    grad_gate, grad_up, grad_down, keep, send = feed_grads(normed_two, dy, down_full, hidden, dgate, dup)
    output = (middle + collect(keep, send)).astype(BF16)[None]

    (third_grads,) = cut_blocks(
        [grad_gate, grad_up, grad_down], third_blocks, third_orders, third_shapes,
        [(len(third_spots), third_rows, quarter)],
        [(0, columns_rows + n * down_shard, down_shard, w, quarter - w) for n, w in enumerate(down_widths) if w < quarter],
    )
    third_sum = lax.psum_scatter(third_grads, "ctx", scatter_dimension=0, tiled=True)

    dmiddle_norm, grad_gain_two = norm_back(middle, gain_two, dnormed_two)
    dmiddle = dlayer + dmiddle_norm
    dm = dmiddle.astype(BF16)
    dm_two = jnp.concatenate([dm, plan.swap(dm, core_bit)])
    grad_out = contract_rows(values, dm_two).astype(BF16)
    dvalues = times_transposed(dm_two, out_full).astype(BF16).reshape(2, rows, half)
    dqueries, grad_upkey, grad_upvalue, keep, send = attend_back(
        queries, query_latent, mixed, lse, dvalues, upkey_full, upvalue_full, keys, query_pos, key_pos, 2
    )
    dlatent = reduce_far(plan, keep.astype(F32) + plan.swap(send, y_bit).astype(F32), z_bits)
    dlatent = dlatent.astype(BF16).reshape(2 * rows, latent_half)
    dqueries = dqueries.reshape(2 * rows, half)
    shares = times_transposed(dqueries, query_full) + times_transposed(dlatent, latent_full)
    dnormed_one = shares[:rows] + plan.swap(shares[rows:], core_bit)
    dx_norm, grad_gain_one = norm_back(x_own, gain_one, dnormed_one)
    grad_tokens = (dmiddle + dx_norm).astype(BF16)[None]

    half_order = reduce_order(*half_stages)
    places = [(i, j, m) for i, masks in enumerate(half_order) for j, m in enumerate(masks)]
    owners = [owner_half(me ^ m) for _, _, m in places]
    grad_query = contract_rows(normed_one, dqueries).astype(BF16)
    second_stacks = cut_blocks(
        [grad_query, grad_upkey, grad_upvalue, grad_out],
        [
            [[(i, j, 0, b * half) for i, j, _ in places for b in (0, 1)]],
            [[(i, j, shard, 0) for i, j, _ in places]],
            [[(i, j, shard, pair_width) for i, j, _ in places]],
            [[(i, j, shard + up_shard, 0) for i, j, _ in places]],
        ],
        [[me ^ (m ^ b * core_bit) for _, _, m in places for b in (0, 1)], owners, owners, owners],
        [(shard, [half]), (up_shard, [pair_width]), (up_shard, [pair_width]), (shard, [width])],
        [(len(masks),) + second_message.shape for masks in half_order],
    )
    second_part = reduce_near(plan, second_stacks, y_bit, x_bit)
    grad_latent = contract_rows(normed_one, dlatent).astype(BF16)
    gain_rows = jnp.concatenate([grad_gain_one.reshape(count, shard), grad_gain_two.reshape(count, shard)], 1)
    gain_rows = jnp.pad(gain_rows.astype(BF16)[:, None], ((0, 0), (0, INFO - 1), (0, latent_half - 2 * shard)))
    order = [me ^ (m ^ b * core_bit) for _, _, m in places for b in (0, 1)]
    first_stacks = cut_blocks(
        [grad_latent, gain_rows.reshape(count * INFO, latent_half)],
        [
            [[(i, j, b * band, 0) for i, j, _ in places for b in (0, 1)]],
            [[(i, j, b * band + shard, 0) for i, j, _ in places for b in (0, 1)]],
        ],
        [order, order],
        [(shard, [latent_half]), (INFO, [latent_half])],
        [(len(masks), 2 * band, latent_half) for masks in half_order],
    )
    first_part = reduce_near(plan, first_stacks, y_bit, x_bit)
    first_part, second_part, third_sum = tie(first_part, second_part, third_sum)
    third_sum = reduce_far(plan, third_sum, extra_bits) if extra_bits else third_sum[0] if third_sum.ndim == 3 else third_sum
    down_sum = third_sum[columns_rows:].reshape(2, down_shard, quarter)
    down_sum = jnp.concatenate([down_sum[n, :, :w] for n, w in enumerate(down_widths)], 1)
    grad_w_down = plan.deal(down_sum.astype(F32), [(plan.top // 2, core_bit), (plan.top, cross_bit)])
    column_sum = third_sum[:columns_rows].reshape(4, 2 * shard, quarter)
    got = jnp.stack(
        [column_sum[0]] + [plan.swap(column_sum[n].astype(BF16), m).astype(third_sum.dtype) for n, m in enumerate(split_masks) if n]
    )
    grad_columns = jnp.concatenate(
        [lax.dynamic_index_in_dim(got, split ^ n, 0, keepdims=False) for n in range(4)], 1
    ).astype(F32)
    grad_w_gate, grad_w_up = grad_columns[:shard], grad_columns[shard:]
    first_sum = reduce_far(plan, first_part, half_far)
    second_sum = reduce_far(plan, second_part, half_far)
    own, got = second_sum[:shard, :half], plan.swap(second_sum[:shard, half:].astype(BF16), core_bit).astype(F32)
    grad_w_query = jnp.concatenate([jnp.where(core == 0, own, got), jnp.where(core == 0, got, own)], 1)
    dealt = plan.deal(second_sum[shard:].astype(BF16), [(plan.top, core_bit)]).astype(F32)
    grad_w_out = dealt[up_shard:]
    own, got = first_sum[:band], plan.swap(first_sum[band:].astype(BF16), core_bit).astype(F32)
    grad_w_latent = jnp.concatenate([jnp.where(core == 0, own, got), jnp.where(core == 0, got, own)], 1)[:shard]
    gain_sums = own[shard] + got[shard]

    return (
        output, grad_tokens, gain_sums[:shard], gain_sums[shard : 2 * shard],
        grad_w_query, grad_w_latent, dealt[:up_shard, :pair_width], dealt[:up_shard, pair_width:],
        grad_w_out, grad_w_gate, grad_w_up, grad_w_down,
    )


def solution(mesh):
    rows = P(("dp", "ctx"), None)
    vector = P(("dp", "ctx"))
    stretch = P("dp", "ctx", None)
    in_specs = (stretch, stretch, P("dp"), P(), P("dp", "ctx"), vector, vector) + (rows,) * 8
    out_specs = (stretch, stretch, vector, vector) + (rows,) * 8
    return jax.shard_map(
        functools.partial(per_device, Plan(mesh)), mesh=mesh, in_specs=in_specs, out_specs=out_specs,
        check_vma=False,
    )
```

```python
import functools
import itertools
import math

import jax
import jax.numpy as jnp
from jax import lax
from jax.experimental import pallas as pl
from jax.experimental.pallas import tpu as pltpu
from jax.sharding import PartitionSpec as P

PAIRS_A_STEP = 2
HEAD = 64
LATENT = 256
DOMAINS = 8
EPS = 1e-06
SCALE = 0.125
MASKED = -1e30
AXES = ("dp", "ctx")
BF16 = jnp.bfloat16
F32 = jnp.float32
INFO = 8
VMEM_BYTES = 56 * 1024 * 1024


def product(left, right):
    return jnp.dot(left, right, preferred_element_type=F32)


def contract_rows(left, right):
    return lax.dot_general(left, right, (((0,), (0,)), ((), ())), preferred_element_type=F32)


def times_transposed(left, right):
    return lax.dot_general(left, right, (((1,), (1,)), ((), ())), preferred_element_type=F32)


def inverse_rms(rows):
    return lax.rsqrt(jnp.mean(rows * rows, -1, keepdims=True) + EPS)


def norm_back(rows, gain, grad):
    r = inverse_rms(rows)
    grad_gain = jnp.sum(grad * rows * r, 0)
    scaled = grad * gain
    mean = jnp.mean(scaled * rows, -1, keepdims=True)
    return r * scaled - rows * (r * r * r * mean), grad_gain


def groups_of(spots):
    groups = {}
    for n, (i, j, r, k) in enumerate(spots):
        groups.setdefault((i, r, k), []).append((j, n))
    return [(key, [n for _, n in sorted(found)]) for key, found in groups.items()]


def permute_blocks(chosen, stack):
    out = product(chosen.astype(BF16), stack.reshape(stack.shape[0], -1)).astype(BF16)
    return out.reshape(-1, *stack.shape[1:])


def bands_of(widths):
    return list(zip(widths, itertools.accumulate([0, *widths[:-1]])))


def kernel_bytes(shapes):
    return 4 * sum(math.prod(shape) for shape in shapes) + (4 << 20)


def place_blocks(pieces, blocks, orders, shapes):
    if any(rows % 8 for rows, _ in shapes):
        made = []
        for (rows, widths), bands, order in zip(shapes, blocks, orders):
            parts = []
            for (width, _), spots in zip(bands_of(widths), bands):
                groups = groups_of(spots)
                stack = jnp.concatenate([pieces[i][:, r : r + rows, k : k + width] for (i, r, k), _ in groups])
                own = jnp.stack([order[n] for _, ns in groups for n in ns])
                numbers = jnp.arange(len(spots), dtype=own.dtype)
                parts.append(permute_blocks(own[None, :] == numbers[:, None], stack))
            made.append(jnp.concatenate(parts, 2).reshape(-1, sum(widths)))
        return made

    def kernel(order_ref, *refs):
        sources, targets = refs[: len(pieces)], refs[len(pieces) :]
        first = 0
        for target, (rows, widths), bands in zip(targets, shapes, blocks):
            for (width, column), spots in zip(bands_of(widths), bands):
                for n, (i, j, r, k) in enumerate(spots):
                    target[order_ref[first + n], :, column : column + width] = sources[i][
                        j, r : r + rows, k : k + width
                    ]
            first += len(bands[0])

    out_shapes = [(len(bands[0]), rows, sum(widths)) for (rows, widths), bands in zip(shapes, blocks)]
    made = pl.pallas_call(
        kernel,
        out_shape=[jax.ShapeDtypeStruct(shape, BF16) for shape in out_shapes],
        in_specs=[pl.BlockSpec(memory_space=pltpu.SMEM)]
        + [pl.BlockSpec(memory_space=pltpu.VMEM)] * len(pieces),
        out_specs=[pl.BlockSpec(memory_space=pltpu.VMEM)] * len(shapes),
        compiler_params=pltpu.CompilerParams(
            vmem_limit_bytes=kernel_bytes(out_shapes + [p.shape for p in pieces])
        ),
        name="place_blocks",
    )(jnp.stack([n for order in orders for n in order]), *pieces)
    return [whole.reshape(-1, whole.shape[-1]) for whole in made]


def cut_blocks(matrices, blocks, orders, shapes, piece_shapes, spare=()):
    if any(rows % 8 for rows, _ in shapes):
        bands_at = [{} for _ in piece_shapes]
        for (rows, widths), bands, order, matrix in zip(shapes, blocks, orders, matrices):
            grid = matrix.reshape(len(bands[0]), rows, -1)
            for (width, column), spots in zip(bands_of(widths), bands):
                for (i, r, k), ns in groups_of(spots):
                    own = jnp.stack([order[n] for n in ns])
                    chosen = own[:, None] == jnp.arange(len(spots), dtype=own.dtype)[None, :]
                    bands_at[i].setdefault(r, {})[k] = permute_blocks(chosen, grid[:, :, column : column + width])
        for i, r, rows, k, columns in spare:
            bands_at[i].setdefault(r, {})[k] = jnp.zeros((piece_shapes[i][0], rows, columns), BF16)
        return [
            jnp.concatenate(
                [jnp.concatenate([row[k] for k in sorted(row)], 2) for _, row in sorted(band.items())], 1
            )
            for band in bands_at
        ]

    def kernel(order_ref, *refs):
        sources, targets = refs[: len(matrices)], refs[len(matrices) :]
        for i, r, rows, k, columns in spare:
            targets[i][:, r : r + rows, k : k + columns] = jnp.zeros((piece_shapes[i][0], rows, columns), BF16)
        first = 0
        for source, (rows, widths), bands in zip(sources, shapes, blocks):
            for (width, column), spots in zip(bands_of(widths), bands):
                for n, (i, j, r, k) in enumerate(spots):
                    targets[i][j, r : r + rows, k : k + width] = source[
                        order_ref[first + n], :, column : column + width
                    ]
            first += len(bands[0])

    grids = [matrix.reshape(-1, rows, matrix.shape[-1]) for matrix, (rows, _) in zip(matrices, shapes)]
    return pl.pallas_call(
        kernel,
        out_shape=[jax.ShapeDtypeStruct(shape, BF16) for shape in piece_shapes],
        in_specs=[pl.BlockSpec(memory_space=pltpu.SMEM)]
        + [pl.BlockSpec(memory_space=pltpu.VMEM)] * len(matrices),
        out_specs=[pl.BlockSpec(memory_space=pltpu.VMEM)] * len(piece_shapes),
        compiler_params=pltpu.CompilerParams(
            vmem_limit_bytes=kernel_bytes(list(piece_shapes) + [g.shape for g in grids])
        ),
        name="cut_blocks",
    )(jnp.stack([n for order in orders for n in order]), *grids)


def pair_scores(query_latent, keys, visible):
    scores = times_transposed(query_latent * jnp.asarray(SCALE, BF16), keys)
    return jnp.where(visible, scores, MASKED)


def visible_keys(query_pos, key_pos):
    return jnp.concatenate([query_pos, query_pos], 0) >= key_pos


def pair_lanes(n):
    return slice(2 * n * HEAD, 2 * (n + 1) * HEAD)


def attend_kernel(q_ref, uk_ref, uv_ref, keys_ref, qpos_ref, kpos_ref, ql_ref, mixed_ref, lse_ref, values_ref):
    keys = keys_ref[0]
    visible = visible_keys(qpos_ref[0], kpos_ref[0])
    for n in range(ql_ref.shape[1]):
        lanes = pair_lanes(n)
        q, uk, uv = q_ref[0][:, lanes], uk_ref[:, lanes], uv_ref[:, lanes]
        rows = q.shape[0]
        ql = jnp.concatenate(
            [times_transposed(q[:, k : k + HEAD], uk[:, k : k + HEAD]) for k in (0, HEAD)], 0
        ).astype(BF16)
        scores = pair_scores(ql, keys, visible)
        top = jnp.max(scores, -1, keepdims=True)
        terms = jnp.exp(scores - top)
        total = jnp.sum(terms, -1, keepdims=True)
        probs = (terms * (1.0 / total)).astype(BF16)
        mixed = product(probs, keys).astype(BF16)
        ql_ref[0, n] = ql
        mixed_ref[0, n] = mixed
        lse_ref[0, n] = top + jnp.log(total)
        values_ref[0, :, lanes] = jnp.concatenate(
            [product(mixed[:rows], uv[:, :HEAD]), product(mixed[rows:], uv[:, HEAD:])], 1
        ).astype(BF16)


def attend_back_kernel(
    q_ref, ql_ref, mixed_ref, lse_ref, dval_ref, uk_ref, uv_ref, keys_ref, qpos_ref, kpos_ref,
    dq_ref, guk_ref, guv_ref, *rest,
):
    dkeys_refs, (keys_acc, uk_acc, uv_acc) = rest[:-3], rest[-3:]
    seq, step = pl.program_id(0), pl.program_id(1)
    keys = keys_ref[0]
    visible = visible_keys(qpos_ref[0], kpos_ref[0])
    halves = (0, HEAD)
    inside = ql_ref.shape[1]
    dkeys = None
    for n in range(inside):
        lanes = pair_lanes(n)
        q, dval, uk, uv = q_ref[0][:, lanes], dval_ref[0][:, lanes], uk_ref[:, lanes], uv_ref[:, lanes]
        ql, mixed = ql_ref[0, n], mixed_ref[0, n]
        rows = q.shape[0]
        scores = pair_scores(ql, keys, visible)
        probs = jnp.exp(scores - lse_ref[0, n])
        dmixed = jnp.concatenate(
            [times_transposed(dval[:, k : k + HEAD], uv[:, k : k + HEAD]) for k in halves], 0
        ).astype(BF16)
        dprobs = times_transposed(dmixed, keys)
        dscores = probs * (dprobs - jnp.sum(probs * dprobs, -1, keepdims=True))
        dscores = dscores.astype(BF16) * jnp.asarray(SCALE, BF16)
        dql = product(dscores, keys).astype(BF16)
        part = contract_rows(dscores, ql) + contract_rows(probs.astype(BF16), dmixed)
        dkeys = part if dkeys is None else dkeys + part
        guk = jnp.concatenate(
            [contract_rows(dql[i * rows : (i + 1) * rows], q[:, k : k + HEAD]) for i, k in enumerate(halves)], 1
        )
        guv = jnp.concatenate(
            [contract_rows(mixed[i * rows : (i + 1) * rows], dval[:, k : k + HEAD]) for i, k in enumerate(halves)], 1
        )
        pair = step * inside + n
        uk_acc[pair] = jnp.where(seq == 0, guk, uk_acc[pair] + guk)
        uv_acc[pair] = jnp.where(seq == 0, guv, uv_acc[pair] + guv)
        dq_ref[0, :, lanes] = jnp.concatenate(
            [product(dql[i * rows : (i + 1) * rows], uk[:, k : k + HEAD]) for i, k in enumerate(halves)], 1
        ).astype(BF16)

    @pl.when(step == 0)
    def _():
        keys_acc[...] = dkeys

    @pl.when(step > 0)
    def _():
        keys_acc[...] += dkeys

    last = pl.num_programs(1) - 1

    @pl.when(step == last)
    def _():
        count = dkeys_refs[0].shape[0]
        for n, ref in enumerate(dkeys_refs):
            part = keys_acc[n * count * rows : (n + 1) * count * rows, :]
            ref[:, 0] = part.reshape(count, rows, LATENT).astype(BF16)

    @pl.when((step == last) & (seq == pl.num_programs(0) - 1))
    def _():
        for n in range(uk_acc.shape[0]):
            guk_ref[:, pair_lanes(n)] = uk_acc[n].astype(BF16)
            guv_ref[:, pair_lanes(n)] = uv_acc[n].astype(BF16)


def attention_specs(length, rows):
    pair = pl.BlockSpec((1, rows, 2 * PAIRS_A_STEP * HEAD), lambda s, p: (s, 0, p))
    up = pl.BlockSpec((LATENT, 2 * PAIRS_A_STEP * HEAD), lambda s, p: (0, p))
    keys = pl.BlockSpec((1, length, LATENT), lambda s, p: (s, 0, 0))
    query_pos = pl.BlockSpec((1, rows, 1), lambda s, p: (s, 0, 0))
    key_pos = pl.BlockSpec((1, 1, length), lambda s, p: (s, 0, 0))
    wide = pl.BlockSpec((1, PAIRS_A_STEP, 2 * rows, LATENT), lambda s, p: (s, p, 0, 0))
    thin = pl.BlockSpec((1, PAIRS_A_STEP, 2 * rows, 1), lambda s, p: (s, p, 0, 0))
    return pair, up, keys, query_pos, key_pos, wide, thin


def attend(q, uk, uv, keys, query_pos, key_pos):
    seqs, length, _ = keys.shape
    rows, pairs = q.shape[1], q.shape[2] // (2 * HEAD)
    pair, up, key, qpos, kpos, wide, thin = attention_specs(length, rows)
    flops = seqs * pairs * 2 * rows * length * LATENT * 4
    return pl.pallas_call(
        attend_kernel,
        grid=(seqs, pairs // PAIRS_A_STEP),
        in_specs=[pair, up, up, key, qpos, kpos],
        out_specs=[wide, wide, thin, pair],
        out_shape=[
            jax.ShapeDtypeStruct((seqs, pairs, 2 * rows, LATENT), BF16),
            jax.ShapeDtypeStruct((seqs, pairs, 2 * rows, LATENT), BF16),
            jax.ShapeDtypeStruct((seqs, pairs, 2 * rows, 1), F32),
            jax.ShapeDtypeStruct(q.shape, BF16),
        ],
        compiler_params=pltpu.CompilerParams(vmem_limit_bytes=VMEM_BYTES),
        cost_estimate=pl.CostEstimate(flops=flops, bytes_accessed=6 << 20, transcendentals=seqs * pairs * 2 * rows * length),
        name="attend",
    )(q, uk, uv, keys, query_pos, key_pos)


def attend_back(q, ql, mixed, lse, dval, uk, uv, keys, query_pos, key_pos, parts):
    seqs, length, _ = keys.shape
    rows, pairs = q.shape[1], q.shape[2] // (2 * HEAD)
    pair, up, key, qpos, kpos, wide, thin = attention_specs(length, rows)
    whole = pl.BlockSpec(uk.shape, lambda s, p: (0, 0))
    count = length // rows // parts
    flops = seqs * pairs * 2 * rows * length * LATENT * 10
    return pl.pallas_call(
        attend_back_kernel,
        grid=(seqs, pairs // PAIRS_A_STEP),
        in_specs=[pair, wide, wide, thin, pair, up, up, key, qpos, kpos],
        out_specs=[pair, whole, whole]
        + [pl.BlockSpec((count, 1, rows, LATENT), lambda s, p: (0, s, 0, 0))] * parts,
        out_shape=[jax.ShapeDtypeStruct(q.shape, BF16)]
        + [jax.ShapeDtypeStruct(uk.shape, BF16)] * 2
        + [jax.ShapeDtypeStruct((count, seqs, rows, LATENT), BF16)] * parts,
        scratch_shapes=[
            pltpu.VMEM((length, LATENT), F32),
            pltpu.VMEM((pairs, LATENT, 2 * HEAD), F32),
            pltpu.VMEM((pairs, LATENT, 2 * HEAD), F32),
        ],
        compiler_params=pltpu.CompilerParams(vmem_limit_bytes=VMEM_BYTES),
        cost_estimate=pl.CostEstimate(flops=flops, bytes_accessed=8 << 20, transcendentals=seqs * pairs * 2 * rows * length),
        name="attend_back",
    )(q, ql, mixed, lse, dval, uk, uv, keys, query_pos, key_pos)


def row_tiles(total, size):
    return [(at, min(size, total - at)) for at in range(0, total, size)]


def feed_kernel(*refs):
    rows_refs, dy_refs = refs[:4], refs[4:8]
    gate_ref, up_ref, down_ref, hidden_ref, dgate_ref, dup_ref, keep_ref, send_ref = refs[8:]
    rows = rows_refs[0].shape[0]
    for pair in (0, 1):
        left = jnp.concatenate([rows_refs[2 * pair][...], rows_refs[2 * pair + 1][...]])
        dy = jnp.concatenate([dy_refs[2 * pair][...], dy_refs[2 * pair + 1][...]])
        gate = product(left, gate_ref[...])
        up = product(left, up_ref[...])
        dhidden = times_transposed(dy, down_ref[...])
        sigmoid = 1.0 / (1.0 + jnp.exp(-gate))
        silu = gate * sigmoid
        span = slice(2 * pair * rows, 2 * (pair + 1) * rows)
        hidden_ref[span] = (silu * up).astype(BF16)
        dgate = (dhidden * up * (sigmoid * (1.0 + gate * (1.0 - sigmoid)))).astype(BF16)
        dup = (dhidden * silu).astype(BF16)
        dgate_ref[span] = dgate
        dup_ref[span] = dup
        shares = times_transposed(dgate, gate_ref[...]) + times_transposed(dup, up_ref[...])
        keep_ref[pair] = shares[:rows]
        send_ref[pair] = shares[rows:]


def feed_grads_kernel(*refs):
    rows_refs, dy_refs = refs[:4], refs[4:8]
    down_ref, hidden_ref, dgate_ref, dup_ref, ggate_ref, gup_ref, gdown_ref, keep_ref, send_ref = refs[8:]
    rows = rows_refs[0].shape[0]
    for at, size in row_tiles(rows_refs[0].shape[1], 256):
        left = jnp.concatenate([ref[:, at : at + size] for ref in rows_refs])
        ggate_ref[at : at + size] = contract_rows(left, dgate_ref[...]).astype(BF16)
        gup_ref[at : at + size] = contract_rows(left, dup_ref[...]).astype(BF16)
    dy = jnp.concatenate([ref[...] for ref in dy_refs])
    for at, size in row_tiles(hidden_ref.shape[1], 256):
        gdown_ref[at : at + size] = contract_rows(hidden_ref[:, at : at + size], dy).astype(BF16)
    for pair in (0, 1):
        shares = product(hidden_ref[2 * pair * rows : 2 * (pair + 1) * rows], down_ref[...])
        keep_ref[pair] = shares[:rows]
        send_ref[pair] = shares[rows:]


def feed(normed, dy, gate_full, up_full, down_full):
    rows, width = normed[0].shape
    units = gate_full.shape[1]
    low = jax.ShapeDtypeStruct((4 * rows, units), BF16)
    share = jax.ShapeDtypeStruct((2, rows, width), F32)
    flops = 2 * 4 * rows * width * units
    return pl.pallas_call(
        feed_kernel,
        out_shape=[low, low, low, share, share],
        in_specs=[pl.BlockSpec(memory_space=pltpu.VMEM)] * 11,
        out_specs=[pl.BlockSpec(memory_space=pltpu.VMEM)] * 5,
        compiler_params=pltpu.CompilerParams(vmem_limit_bytes=40 << 20),
        cost_estimate=pl.CostEstimate(flops=5 * flops, bytes_accessed=11 << 20, transcendentals=4 * rows * units),
        name="feed",
    )(*normed, *dy, gate_full, up_full, down_full)


def feed_grads(normed, dy, down_full, hidden, dgate, dup):
    rows, width = normed[0].shape
    units = hidden.shape[1]
    share = jax.ShapeDtypeStruct((2, rows, width), F32)
    flops = 2 * 4 * rows * width * units
    return pl.pallas_call(
        feed_grads_kernel,
        out_shape=[jax.ShapeDtypeStruct((width, units), BF16)] * 2
        + [jax.ShapeDtypeStruct((units, width), BF16), share, share],
        in_specs=[pl.BlockSpec(memory_space=pltpu.VMEM)] * 12,
        out_specs=[pl.BlockSpec(memory_space=pltpu.VMEM)] * 5,
        compiler_params=pltpu.CompilerParams(vmem_limit_bytes=40 << 20),
        cost_estimate=pl.CostEstimate(flops=4 * flops, bytes_accessed=14 << 20, transcendentals=0),
        name="feed_grads",
    )(*normed, *dy, down_full, hidden, dgate, dup)


class Plan:
    def __init__(self, mesh):
        self.dp, self.ctx = mesh.shape["dp"], mesh.shape["ctx"]
        self.count = self.dp * self.ctx
        self.core = self.ctx
        self.cross = 2 * self.ctx
        top = self.count // 2
        bits = [1 << n for n in range(self.count.bit_length() - 1)]
        ctx_bits = [b for b in bits if b < self.ctx]
        self.half_bits = [b for b in bits if b != self.core]
        self.split_bits = [self.core, self.cross]
        self.quarter_bits = [b for b in bits if b not in self.split_bits]
        self.ctx_bits = ctx_bits
        self.top = top

    def swap(self, value, mask):
        return lax.ppermute(value, AXES, [(n, n ^ mask) for n in range(self.count)])

    def swap_bits(self, number, first, second):
        if first == second:
            return number
        one, two = (number // first) % 2, (number // second) % 2
        return number + (two - one) * first + (one - two) * second

    def deal(self, value, pairs):
        table = []
        for n in range(self.count):
            m = n
            for first, second in pairs:
                m = self.swap_bits(m, first, second)
            table.append((n, m))
        if all(a == b for a, b in table):
            return value
        return lax.ppermute(value, AXES, table)


def masks_of(bits):
    out = [0]
    for bit in bits:
        out = out + [m ^ bit for m in out]
    return out


def gather(plan, value, far, bits, groups):
    done = [([m], value[None] if m == 0 else plan.swap(value, m)[None]) for m in masks_of(far)]
    for bit, count in zip(bits, groups):
        size = -(-len(done) // count)
        sent = []
        for at in range(0, len(done), size):
            some = done[at : at + size]
            masks = [m for ms, _ in some for m in ms]
            stack = some[0][1] if len(some) == 1 else jnp.concatenate([a for _, a in some])
            sent.append(([m ^ bit for m in masks], plan.swap(stack, bit)))
        done = done + sent
    return done


def reduce_order(far, second, first):
    base = masks_of(far)
    return [[m ^ one ^ two for m in base] for one in (0, first) for two in (0, second)]


def reduce_far(plan, part, far):
    total = part[0].astype(F32)
    for n, mask in enumerate(masks_of(far)):
        if n:
            total = total + plan.swap(part[n].astype(BF16), mask).astype(F32)
    return total


def reduce_near(plan, stacks, second, first):
    keep0, keep1, send0, send1 = stacks
    got1 = plan.swap(send1, first)
    got0 = plan.swap(send0, first)
    part1 = (keep1.astype(F32) + got1.astype(F32)).astype(BF16)
    got = plan.swap(part1, second)
    return (keep0.astype(F32) + got0.astype(F32) + got.astype(F32)).astype(BF16)


def tie(*values):
    return lax.optimization_barrier(values)


def per_device(plan, tokens, cotangent, domain_ids, domain_weights, stretch_offsets, gain_attn, gain_ffn,
               w_query, w_latent, w_upkey, w_upvalue, w_out, w_gate, w_up, w_down):
    _, rows, width = tokens.shape
    me = lax.axis_index("dp") * plan.ctx + lax.axis_index("ctx")
    here = lax.axis_index("ctx")
    core = (me // plan.core) % 2
    core_bit, cross_bit = plan.core, plan.cross
    count = plan.count
    shard = w_query.shape[0]
    up_shard = w_upkey.shape[0]
    down_shard = w_down.shape[0]
    half = w_query.shape[1] // 2
    latent_half = w_latent.shape[1] // 2
    pair_width = w_upkey.shape[1]
    quarter = w_gate.shape[1] // 4
    y_bit, *z_bits = plan.ctx_bits
    x_bit = plan.half_bits[-1]
    half_far = [b for b in plan.half_bits if b not in (x_bit, y_bit)]
    extra_bits = [b for b in plan.quarter_bits if b not in plan.ctx_bits]
    half_stages = (half_far, y_bit, x_bit)

    def halves(value, size):
        low, high = value[:, :size], value[:, size:]
        return jnp.where(core == 0, low, high), jnp.where(core == 0, high, low)

    query_own, query_other = halves(w_query, half)
    latent_own, latent_other = halves(w_latent, latent_half)
    info = jnp.concatenate([gain_attn, gain_ffn, stretch_offsets[0].astype(BF16)])
    info = jnp.pad(info[None], ((0, INFO - 1), (0, latent_half - info.shape[0])))
    band = shard + INFO
    folds = half // latent_half
    fold = lambda value: jnp.concatenate(jnp.split(value, folds, 1), 0)
    unfold = lambda value: jnp.concatenate(jnp.split(value, folds, 0), 1)
    got = plan.swap(jnp.concatenate([latent_other, info, fold(query_other)]), core_bit)
    first_message = jnp.concatenate([latent_own, info, got[:band]])
    dealt = plan.deal(
        jnp.concatenate([jnp.concatenate([w_upkey, w_upvalue], 1), w_out]), [(plan.top, core_bit)]
    )
    second_message = jnp.concatenate([jnp.concatenate([query_own, unfold(got[band:])], 1), dealt])
    split_masks = masks_of(plan.split_bits)
    split = (me // core_bit) % 2 + 2 * ((me // cross_bit) % 2)
    columns = jnp.concatenate([w_gate, w_up]).reshape(2 * shard, 4, quarter).transpose(1, 0, 2)

    def quarter_of(mask_index):
        return lax.dynamic_index_in_dim(columns, split ^ mask_index, 0, keepdims=False)

    down = plan.deal(w_down, [(plan.top, cross_bit), (plan.top // 2, core_bit)])
    low_width = min(quarter // 128 * 128, width)
    down_widths = [low_width, width - low_width]

    def narrow(value, column, columns):
        return jnp.pad(value[:, column : column + columns], ((0, 0), (0, quarter - columns)))

    third_message = jnp.concatenate(
        [quarter_of(0)]
        + [plan.swap(quarter_of(n), m) for n, m in enumerate(split_masks) if n]
        + [narrow(down, column, columns) for columns, column in bands_of(down_widths)]
    )
    columns_rows = 8 * shard
    third_rows = third_message.shape[0]

    tokens_two = jnp.concatenate([tokens[0], plan.swap(tokens[0], core_bit)])
    x_two = tokens_two.astype(F32)

    first_pieces = gather(plan, first_message, half_far, (y_bit, x_bit), (1, 1))
    second_pieces = gather(plan, second_message, half_far, (y_bit, x_bit), (4, 1))
    third_stack = jnp.concatenate([a for _, a in gather(plan, third_message, extra_bits, (), ())])
    extra_masks = masks_of(extra_bits)
    third_whole = lax.all_gather(third_stack, "ctx", axis=0, tiled=True)
    third_spots = [(c * len(extra_masks) + e, (me - here + c) ^ m) for c in range(plan.ctx) for e, m in enumerate(extra_masks)]

    def spots(pieces):
        return [(i, j, m) for i, (masks, _) in enumerate(pieces) for j, m in enumerate(masks)]

    def owner_half(number):
        return plan.swap_bits(number, plan.top, core_bit) % (count // 2)

    def owner_quarter(number):
        source = plan.swap_bits(number, plan.top // 2, core_bit)
        return plan.swap_bits(source, plan.top, cross_bit) % (count // 4)

    found = spots(first_pieces)
    (latent_full,) = place_blocks(
        [a for _, a in first_pieces],
        [[[(i, j, b * band, 0) for i, j, _ in found for b in (0, 1)]]],
        [[me ^ (m ^ b * core_bit) for _, _, m in found for b in (0, 1)]],
        [(shard, [latent_half])],
    )
    rows_info = jnp.concatenate(
        [a[:, shard :: band, : 2 * shard + 1] for _, a in first_pieces]
    )

    found = spots(second_pieces)
    owners = [owner_half(me ^ m) for _, _, m in found]
    query_full, upkey_full, upvalue_full, out_full = place_blocks(
        [a for _, a in second_pieces],
        [
            [[(i, j, 0, b * half) for i, j, _ in found for b in (0, 1)]],
            [[(i, j, shard, 0) for i, j, _ in found]],
            [[(i, j, shard, pair_width) for i, j, _ in found]],
            [[(i, j, shard + up_shard, 0) for i, j, _ in found]],
        ],
        [[me ^ (m ^ b * core_bit) for _, _, m in found for b in (0, 1)], owners, owners, owners],
        [(shard, [half]), (up_shard, [pair_width]), (up_shard, [pair_width]), (shard, [width])],
    )

    column_order = [number ^ s for _, number in third_spots for s in split_masks]
    down_order = [owner_quarter(number) for _, number in third_spots]
    third_blocks = [
        [[(0, j, n * 2 * shard, 0) for j, _ in third_spots for n in range(4)]],
        [[(0, j, n * 2 * shard + shard, 0) for j, _ in third_spots for n in range(4)]],
        [[(0, j, columns_rows + n * down_shard, 0) for j, _ in third_spots] for n in (0, 1)],
    ]
    third_orders = [column_order, column_order, down_order]
    third_shapes = [(shard, [quarter]), (shard, [quarter]), (down_shard, down_widths)]
    gate_full, up_full, down_full = place_blocks([third_whole], third_blocks, third_orders, third_shapes)

    masks_info = [m for _, _, m in spots(first_pieces)]
    number = jnp.stack([jnp.stack([me ^ m, me ^ m ^ core_bit]) for m in masks_info]).reshape(-1)
    chosen = (number[:, None] == jnp.arange(count)[None, :]).astype(BF16)
    gains = contract_rows(chosen, rows_info[..., : 2 * shard].reshape(count, 2 * shard))
    gain_one = gains[:, :shard].reshape(width)
    gain_two = gains[:, shard:].reshape(width)
    ctx_masks = [m ^ y for y in (0, y_bit) for m in masks_of(z_bits)]
    offsets = jnp.stack(
        [rows_info[masks_info.index(m), :, 2 * shard] for m in ctx_masks], 1
    ).astype(jnp.int32)
    within = jnp.arange(rows, dtype=jnp.int32)
    key_pos = (offsets[:, :, None] * rows + within).reshape(2, 1, -1)
    query_pos = (offsets[:, :1] * rows + within)[:, :, None]

    normed_one = (x_two * inverse_rms(x_two) * gain_one).astype(BF16)
    latent = product(normed_one, latent_full).astype(BF16)
    latent_message = latent.reshape(2, rows, latent_half)
    key_pieces = gather(plan, latent_message, z_bits, (y_bit,), (4,))
    key_of = {m: a[j] for masks, a in key_pieces for j, m in enumerate(masks)}
    keys = jnp.concatenate([key_of[m] for m in ctx_masks], 1)
    queries = product(normed_one, query_full).astype(BF16).reshape(2, rows, half)
    query_latent, mixed, lse, values = attend(queries, upkey_full, upvalue_full, keys, query_pos, key_pos)
    values = values.reshape(2 * rows, half)
    shares = product(values, out_full)
    x_own = x_two[:rows]
    middle = x_own + shares[:rows] + plan.swap(shares[rows:], core_bit)

    def spread(value):
        near = plan.swap(value, core_bit)
        across = plan.swap(value, cross_bit)
        return [value, near, across, plan.swap(across, core_bit)]

    def collect(keep, send):
        got = plan.swap(send, core_bit)
        across = plan.swap((keep[1] + got[1]).astype(BF16), cross_bit)
        return keep[0] + got[0] + across.astype(F32)

    match = domain_ids[:, None] == jnp.arange(DOMAINS, dtype=jnp.int32)[None, :]
    scale = jnp.sum(jnp.where(match, domain_weights[None, :], 0.0))
    dlayer = cotangent[0].astype(F32) * scale
    dy = spread(dlayer.astype(BF16))

    normed_two = spread((middle * inverse_rms(middle) * gain_two).astype(BF16))
    hidden, dgate, dup, keep, send = feed(normed_two, dy, gate_full, up_full, down_full)
    dnormed_two = collect(keep, send)
    grad_gate, grad_up, grad_down, keep, send = feed_grads(normed_two, dy, down_full, hidden, dgate, dup)
    output = (middle + collect(keep, send)).astype(BF16)[None]

    (third_grads,) = cut_blocks(
        [grad_gate, grad_up, grad_down], third_blocks, third_orders, third_shapes,
        [(len(third_spots), third_rows, quarter)],
        [(0, columns_rows + n * down_shard, down_shard, w, quarter - w) for n, w in enumerate(down_widths) if w < quarter],
    )
    third_sum = lax.psum_scatter(third_grads, "ctx", scatter_dimension=0, tiled=True)

    dmiddle_norm, grad_gain_two = norm_back(middle, gain_two, dnormed_two)
    dmiddle = dlayer + dmiddle_norm
    dm = dmiddle.astype(BF16)
    dm_two = jnp.concatenate([dm, plan.swap(dm, core_bit)])
    grad_out = contract_rows(values, dm_two).astype(BF16)
    dvalues = times_transposed(dm_two, out_full).astype(BF16).reshape(2, rows, half)
    dqueries, grad_upkey, grad_upvalue, keep, send = attend_back(
        queries, query_latent, mixed, lse, dvalues, upkey_full, upvalue_full, keys, query_pos, key_pos, 2
    )
    dlatent = reduce_far(plan, keep.astype(F32) + plan.swap(send, y_bit).astype(F32), z_bits)
    dlatent = dlatent.astype(BF16).reshape(2 * rows, latent_half)
    dqueries = dqueries.reshape(2 * rows, half)
    shares = times_transposed(dqueries, query_full) + times_transposed(dlatent, latent_full)
    dnormed_one = shares[:rows] + plan.swap(shares[rows:], core_bit)
    dx_norm, grad_gain_one = norm_back(x_own, gain_one, dnormed_one)
    grad_tokens = (dmiddle + dx_norm).astype(BF16)[None]

    half_order = reduce_order(*half_stages)
    places = [(i, j, m) for i, masks in enumerate(half_order) for j, m in enumerate(masks)]
    owners = [owner_half(me ^ m) for _, _, m in places]
    grad_query = contract_rows(normed_one, dqueries).astype(BF16)
    second_stacks = cut_blocks(
        [grad_query, grad_upkey, grad_upvalue, grad_out],
        [
            [[(i, j, 0, b * half) for i, j, _ in places for b in (0, 1)]],
            [[(i, j, shard, 0) for i, j, _ in places]],
            [[(i, j, shard, pair_width) for i, j, _ in places]],
            [[(i, j, shard + up_shard, 0) for i, j, _ in places]],
        ],
        [[me ^ (m ^ b * core_bit) for _, _, m in places for b in (0, 1)], owners, owners, owners],
        [(shard, [half]), (up_shard, [pair_width]), (up_shard, [pair_width]), (shard, [width])],
        [(len(masks),) + second_message.shape for masks in half_order],
    )
    second_part = reduce_near(plan, second_stacks, y_bit, x_bit)
    grad_latent = contract_rows(normed_one, dlatent).astype(BF16)
    gain_rows = jnp.concatenate([grad_gain_one.reshape(count, shard), grad_gain_two.reshape(count, shard)], 1)
    gain_rows = jnp.pad(gain_rows.astype(BF16)[:, None], ((0, 0), (0, INFO - 1), (0, latent_half - 2 * shard)))
    order = [me ^ (m ^ b * core_bit) for _, _, m in places for b in (0, 1)]
    first_stacks = cut_blocks(
        [grad_latent, gain_rows.reshape(count * INFO, latent_half)],
        [
            [[(i, j, b * band, 0) for i, j, _ in places for b in (0, 1)]],
            [[(i, j, b * band + shard, 0) for i, j, _ in places for b in (0, 1)]],
        ],
        [order, order],
        [(shard, [latent_half]), (INFO, [latent_half])],
        [(len(masks), 2 * band, latent_half) for masks in half_order],
    )
    first_part = reduce_near(plan, first_stacks, y_bit, x_bit)
    first_part, second_part, third_sum = tie(first_part, second_part, third_sum)
    third_sum = reduce_far(plan, third_sum, extra_bits) if extra_bits else third_sum[0] if third_sum.ndim == 3 else third_sum
    down_sum = third_sum[columns_rows:].reshape(2, down_shard, quarter)
    down_sum = jnp.concatenate([down_sum[n, :, :w] for n, w in enumerate(down_widths)], 1)
    grad_w_down = plan.deal(down_sum.astype(F32), [(plan.top // 2, core_bit), (plan.top, cross_bit)])
    column_sum = third_sum[:columns_rows].reshape(4, 2 * shard, quarter)
    got = jnp.stack(
        [column_sum[0]] + [plan.swap(column_sum[n].astype(BF16), m).astype(third_sum.dtype) for n, m in enumerate(split_masks) if n]
    )
    grad_columns = jnp.concatenate(
        [lax.dynamic_index_in_dim(got, split ^ n, 0, keepdims=False) for n in range(4)], 1
    ).astype(F32)
    grad_w_gate, grad_w_up = grad_columns[:shard], grad_columns[shard:]
    first_sum = reduce_far(plan, first_part, half_far)
    second_sum = reduce_far(plan, second_part, half_far)
    own, got = second_sum[:shard, :half], plan.swap(second_sum[:shard, half:].astype(BF16), core_bit).astype(F32)
    grad_w_query = jnp.concatenate([jnp.where(core == 0, own, got), jnp.where(core == 0, got, own)], 1)
    dealt = plan.deal(second_sum[shard:].astype(BF16), [(plan.top, core_bit)]).astype(F32)
    grad_w_out = dealt[up_shard:]
    own, got = first_sum[:band], plan.swap(first_sum[band:].astype(BF16), core_bit).astype(F32)
    grad_w_latent = jnp.concatenate([jnp.where(core == 0, own, got), jnp.where(core == 0, got, own)], 1)[:shard]
    gain_sums = own[shard] + got[shard]

    return (
        output, grad_tokens, gain_sums[:shard], gain_sums[shard : 2 * shard],
        grad_w_query, grad_w_latent, dealt[:up_shard, :pair_width], dealt[:up_shard, pair_width:],
        grad_w_out, grad_w_gate, grad_w_up, grad_w_down,
    )


def solution(mesh):
    rows = P(("dp", "ctx"), None)
    vector = P(("dp", "ctx"))
    stretch = P("dp", "ctx", None)
    in_specs = (stretch, stretch, P("dp"), P(), P("dp", "ctx"), vector, vector) + (rows,) * 8
    out_specs = (stretch, stretch, vector, vector) + (rows,) * 8
    return jax.shard_map(
        functools.partial(per_device, Plan(mesh)), mesh=mesh, in_specs=in_specs, out_specs=out_specs,
        check_vma=False,
    )
```
